32 devices in a mesh: vocab: 8 (over y, x, core), dp: 4 (over z).
Axes of the slice: x: 2, y: 2, z: 4, core: 2. Of those that a mesh axis runs over, the one named last changes fastest.
Arguments:
- token_ids: int32 [32768], P(('vocab', 'dp')), may hold values from 0 to 262143, as said below
- counts: int32 [32], P(('vocab', 'dp')), may hold values from 256 to 1024, as said below
- table: bfloat16 [262144, 128], P(('vocab', 'dp')), may hold values from -6 to 6
- projection: bfloat16 [128, 4096], replicated, may hold values from -0.5 to 0.5
- cotangent: bfloat16 [32768, 4096], P(('vocab', 'dp')), may hold values from -4 to 4
Outputs:
- hidden: bfloat16 [32768, 4096], P(('vocab', 'dp'))
- grad_projection: float32 [128, 4096], replicated
- grad_table: float32 [262144, 128], P(('vocab', 'dp'))
The draws below stay inside these ranges and needn't reach their ends.
Inputs may be any that keep to these rules, and one draw needn't show every extreme that they name: `token_ids`: on each device at most 64 tokens have ids in the rows of any one device, and in every draw one device's rows receive exactly 64 tokens from every device; which rows are frequent is drawn from the seed. `counts`: in every draw some device has all 1024 tokens live.
All inputs are finite; a program needn't handle non-finite values.
Results may differ from the reference program's by a relative error of at most 0.0029.
Values may be sent and summed in bfloat16 or wider, within the bound.
A program may use at most 128 MiB of HBM per device.

```python
import jax
import jax.numpy as jnp
from jax import lax

E = 128
H = 4096
V_DEV = 8192
TOK_DEV = 1024
VOCAB = 262144
TOKENS = 32768
CAP = 64
DEVICES = 32


def draw_token_ids(key, part):
    base = jax.random.fold_in(key, 11)
    hot_owner = jax.random.randint(jax.random.fold_in(base, 1), (), 0, DEVICES)
    owner_shift = jax.random.randint(jax.random.fold_in(base, 2), (DEVICES,), 0, 7)
    row_mult = 2 * jax.random.randint(jax.random.fold_in(base, 3), (), 0, 16384) + 1
    row_add = jax.random.randint(jax.random.fold_in(base, 4), (), 0, V_DEV)
    slots = DEVICES * CAP
    slot_place = jnp.arange(slots, dtype=jnp.int32)
    slot_owner = slot_place // CAP

    def one_device(device):
        inner = jax.random.fold_in(base, 100 + device)
        first, second, third, fourth = jax.random.split(inner, 4)
        raw = jax.random.randint(first, (slots,), 0, 65536)
        score = (raw >> owner_shift[slot_owner]) * slots + slot_place
        score = score + jnp.where(slot_owner == hot_owner, 1 << 29, 0)
        picked = lax.top_k(score, TOK_DEV)[1]
        owner = picked // CAP
        start = jax.random.randint(second, (TOK_DEV,), 0, V_DEV)
        shifts = jax.random.randint(third, (TOK_DEV,), 0, 9)
        local_row = ((start >> shifts) * row_mult + row_add) % V_DEV
        identity = owner * V_DEV + local_row
        order = jax.random.permutation(fourth, TOK_DEV)
        return identity[order].astype(jnp.int32)
    return jax.vmap(one_device)(jnp.arange(DEVICES, dtype=jnp.int32)).reshape(-1)


def draw_counts(key, part):
    drawn = jax.random.randint(jax.random.fold_in(key, 21), (DEVICES,), TOK_DEV // 4, TOK_DEV + 1)
    full_device = jax.random.randint(jax.random.fold_in(key, 22), (), 0, DEVICES)
    return jnp.where(jnp.arange(DEVICES) == full_device, TOK_DEV, drawn).astype(jnp.int32)


def shard_levels(key, dims, cuts, low, top_value):
    level, own = 1.0, jax.random.fold_in(key, 6)
    for axis_at, parts in cuts:
        steps = jnp.exp(jax.random.uniform(jax.random.fold_in(own, axis_at), (parts,), jnp.float32, low / len(cuts), top_value / len(cuts)))
        level = level * jnp.repeat(steps, dims[axis_at] // parts).reshape([-1 if axis == axis_at else 1 for axis in range(len(dims))])
    return level


def normal_values(rng, dims, width, bound, shards=(), held_as=jnp.bfloat16):
    entries = width * jax.random.normal(rng, dims, jnp.float32)
    if shards:
        entries = entries * shard_levels(rng, dims, shards, -0.22, 0.18)
    return jnp.clip(entries, -bound, bound).astype(held_as)


def setup_inputs(seed: int = 0) -> dict:
    streams_of = jax.random.split(jax.random.key(seed), 6)
    token_ids = draw_token_ids(jax.random.fold_in(streams_of[5], 71), 0)
    counts = draw_counts(jax.random.fold_in(streams_of[5], 71), 0)
    table = normal_values(streams_of[2], (VOCAB, E), 1.0, 6.0, ((0, 32),))
    projection = normal_values(streams_of[3], (E, H), E ** -0.5, 0.5)
    cotangent = normal_values(streams_of[4], (TOKENS, H), 0.25, 4.0, ((0, 32),))
    return {"token_ids": token_ids, "counts": counts, "table": table, "projection": projection, "cotangent": cotangent}


def reference(token_ids, counts, table, projection, cotangent):
    position = jnp.arange(TOKENS, dtype=jnp.int32)
    holder = position // TOK_DEV
    live = (position - holder * TOK_DEV) < counts[holder]
    embedded = table[token_ids]
    product = jnp.dot(embedded, projection, preferred_element_type=jnp.float32)
    hidden = jnp.where(live[:, None], product, 0.0).astype(jnp.bfloat16)
    masked = jnp.where(live[:, None], cotangent, jnp.zeros_like(cotangent))
    terms = lax.dot_general(embedded, masked, (((0,), (0,)), ((), ())), preferred_element_type=jnp.float32)
    grad_projection = terms * (1.0 / (TOKENS ** 0.5))
    token_grad = lax.dot_general(masked, projection, (((1,), (1,)), ((), ())), preferred_element_type=jnp.float32).astype(jnp.bfloat16)
    grad_table = jax.ops.segment_sum(token_grad.astype(jnp.float32), token_ids, num_segments=VOCAB)
    return hidden, grad_projection, grad_table
```

```python
import functools
import math

import jax
import jax.numpy as jnp
from jax import lax
from jax.experimental import pallas as pl
from jax.experimental.pallas import tpu as pltpu
from jax.sharding import PartitionSpec as P

AXES = ("vocab", "dp")
ACCS = 4


def exchange(blocks):
    return lax.all_to_all(blocks, AXES, split_axis=0, concat_axis=0, tiled=True)


def scatter_kernel(chunks, rows_ref, incoming_ref, out_ref, acc0, acc1, acc2, acc3, sems):
    accs = (acc0, acc1, acc2, acc3)
    held = acc0.shape[0]
    part = held // chunks
    count = incoming_ref.shape[0]

    def clear(i, carry):
        at = pl.ds(pl.multiple_of(i * 64, 64), 64)
        for acc in accs:
            acc[at, :] = jnp.zeros((64, acc.shape[1]), jnp.float32)
        return carry

    lax.fori_loop(0, held // 64, clear, 0)

    def add(i, carry):
        base = pl.multiple_of(i * 8, 8)
        block = incoming_ref[pl.ds(base, 8), :]
        for j in range(8):
            acc = accs[j % ACCS]
            at = pl.ds(rows_ref[base + j], 1)
            acc[at, :] = acc[at, :] + block[j : j + 1, :]
        return carry

    lax.fori_loop(0, count // 8, add, 0)

    def copy(c):
        at = pl.ds(c * part, part)
        return pltpu.make_async_copy(acc0.at[at, :], out_ref.at[at, :], sems.at[c])

    for c in range(chunks):

        def join(i, carry):
            at = pl.ds(pl.multiple_of(c * part + i * 64, 64), 64)
            acc0[at, :] = (acc0[at, :] + acc1[at, :]) + (acc2[at, :] + acc3[at, :])
            return carry

        lax.fori_loop(0, part // 64, join, 0)
        copy(c).start()
    for c in range(chunks):
        copy(c).wait()


def scatter_rows(rows, incoming, held_rows):
    width = incoming.shape[1]
    chunks = 4
    return pl.pallas_call(
        functools.partial(scatter_kernel, chunks),
        out_shape=jax.ShapeDtypeStruct((held_rows, width), jnp.float32),
        in_specs=[
            pl.BlockSpec(memory_space=pltpu.SMEM),
            pl.BlockSpec(memory_space=pltpu.VMEM),
        ],
        out_specs=pl.BlockSpec(memory_space=pl.ANY),
        scratch_shapes=[pltpu.VMEM((held_rows, width), jnp.float32)] * ACCS
        + [pltpu.SemaphoreType.DMA((chunks,))],
        cost_estimate=pl.CostEstimate(flops=0, bytes_accessed=12 << 20, transcendentals=0),
        name="scatter_rows",
    )(rows, incoming)


def body(token_ids, counts, table, projection, cotangent):
    tokens_here = token_ids.shape[0]
    held_rows = table.shape[0]
    width = table.shape[1]
    hidden_width = projection.shape[1]
    devices_all = lax.axis_size("vocab") * lax.axis_size("dp")
    capacity = max(4, 2 * tokens_here // devices_all)
    slots = devices_all * capacity
    bf16, f32 = jnp.bfloat16, jnp.float32

    owner = token_ids // held_rows
    local_row = token_ids - owner * held_rows
    hits = (owner[:, None] == jnp.arange(devices_all, dtype=jnp.int32)[None, :]).astype(bf16)
    order = jnp.arange(tokens_here, dtype=jnp.int32)
    before = (order[:, None] >= order[None, :]).astype(bf16)
    ranks = jnp.dot(before, hits, preferred_element_type=f32)
    rank = jnp.sum(ranks * hits.astype(f32), axis=1).astype(jnp.int32) - 1
    slot_index = owner * capacity + rank
    place = (slot_index[:, None] == jnp.arange(slots, dtype=jnp.int32)[None, :]).astype(bf16)
    digits = jnp.stack(
        [local_row // 65536, (local_row // 256) % 256, local_row % 256, jnp.ones_like(local_row)]
    ).astype(bf16)
    found = jnp.dot(digits, place, preferred_element_type=f32).astype(jnp.int32)
    requests = found[0] * 65536 + found[1] * 256 + found[2] + found[3] - 1
    requests = jnp.where(found[3] > 0, requests, -1)

    received = exchange(requests.reshape(devices_all, capacity)).reshape(-1)
    valid = received >= 0
    safe_rows = jnp.maximum(received, 0)
    picked = jnp.where(valid[:, None], table[safe_rows], jnp.zeros((1, width), table.dtype))
    returned = exchange(picked.reshape(devices_all, capacity, width)).reshape(-1, width)

    live = order < counts[0]
    masked = jnp.where(live[:, None], cotangent, jnp.zeros_like(cotangent))
    token_grad = lax.dot_general(
        masked, projection, (((1,), (1,)), ((), ())), preferred_element_type=f32
    ).astype(bf16)
    outgoing = lax.dot_general(
        place, token_grad, (((0,), (0,)), ((), ())), preferred_element_type=f32
    ).astype(bf16)
    incoming = exchange(outgoing.reshape(devices_all, capacity, width)).reshape(-1, width)

    embedded = jnp.dot(place, returned, preferred_element_type=f32).astype(bf16)
    terms = lax.dot_general(
        masked, embedded, (((0,), (0,)), ((), ())), preferred_element_type=f32
    ).astype(bf16)
    share = hidden_width // devices_all
    parts = exchange(terms.reshape(devices_all, share, width))
    scaling = 1.0 / math.sqrt(tokens_here * devices_all)
    summed = (jnp.sum(parts.astype(f32), axis=0) * scaling).astype(bf16)
    spread = exchange(jnp.broadcast_to(summed[None], (devices_all, share, width)))
    grad_projection = spread.reshape(hidden_width, width).T.astype(f32)

    product = jnp.dot(embedded, projection, preferred_element_type=f32)
    hidden = jnp.where(live[:, None], product, 0.0).astype(bf16)
    grad_table = scatter_rows(safe_rows, incoming.astype(f32), held_rows)
    return (hidden, grad_projection, grad_table)


def solution(mesh):
    return jax.shard_map(
        body,
        mesh=mesh,
        in_specs=(
            P(AXES),
            P(AXES),
            P(AXES, None),
            P(),
            P(AXES, None),
        ),
        out_specs=(P(AXES, None), P(), P(AXES, None)),
        check_vma=False,
    )
```

```python
import functools
import math

import jax
import jax.numpy as jnp
from jax import lax
from jax.experimental import pallas as pl
from jax.experimental.pallas import tpu as pltpu
from jax.sharding import PartitionSpec as P

AXES = ("vocab", "dp")
ACCS = 4


def exchange(blocks):
    return lax.all_to_all(blocks, AXES, split_axis=0, concat_axis=0, tiled=True)


def scatter_kernel(chunks, rows_ref, incoming_ref, out_ref, acc0, acc1, acc2, acc3, sems):
    accs = (acc0, acc1, acc2, acc3)
    held = acc0.shape[0]
    part = held // chunks
    count = incoming_ref.shape[0]

    def clear(i, carry):
        at = pl.ds(pl.multiple_of(i * 64, 64), 64)
        for acc in accs:
            acc[at, :] = jnp.zeros((64, acc.shape[1]), jnp.float32)
        return carry

    lax.fori_loop(0, held // 64, clear, 0)

    def add(i, carry):
        base = pl.multiple_of(i * 8, 8)
        block = incoming_ref[pl.ds(base, 8), :]
        for j in range(8):
            acc = accs[j % ACCS]
            at = pl.ds(rows_ref[base + j], 1)
            acc[at, :] = acc[at, :] + block[j : j + 1, :]
        return carry

    lax.fori_loop(0, count // 8, add, 0)

    def copy(c):
        at = pl.ds(c * part, part)
        return pltpu.make_async_copy(acc0.at[at, :], out_ref.at[at, :], sems.at[c])

    for c in range(chunks):

        def join(i, carry):
            at = pl.ds(pl.multiple_of(c * part + i * 64, 64), 64)
            acc0[at, :] = (acc0[at, :] + acc1[at, :]) + (acc2[at, :] + acc3[at, :])
            return carry

        lax.fori_loop(0, part // 64, join, 0)
        copy(c).start()
    for c in range(chunks):
        copy(c).wait()


def scatter_rows(rows, incoming, held_rows):
    width = incoming.shape[1]
    chunks = 4
    return pl.pallas_call(
        functools.partial(scatter_kernel, chunks),
        out_shape=jax.ShapeDtypeStruct((held_rows, width), jnp.float32),
        in_specs=[
            pl.BlockSpec(memory_space=pltpu.SMEM),
            pl.BlockSpec(memory_space=pltpu.VMEM),
        ],
        out_specs=pl.BlockSpec(memory_space=pl.ANY),
        scratch_shapes=[pltpu.VMEM((held_rows, width), jnp.float32)] * ACCS
        + [pltpu.SemaphoreType.DMA((chunks,))],
        cost_estimate=pl.CostEstimate(flops=0, bytes_accessed=12 << 20, transcendentals=0),
        name="scatter_rows",
    )(rows, incoming)

MESH = pl.DeviceIdType.MESH
LANES = 128


def remote(src, dst, send_sem, recv_sem, where):
    return pltpu.make_async_remote_copy(
        src_ref=src, dst_ref=dst, send_sem=send_sem, recv_sem=recv_sem,
        device_id=where, device_id_type=MESH,
    )


def reduce_kernel(
    n_vocab, n_dp, split, scaling, emb_ref, cot_ref, out_ref,
    cot_buf, emb_t, send_a, recv_a, acc_a, send_b, recv_b, acc_b, recv_c, full,
    load_sem, sa, ra, sb, rb, sc, rc, sd, rd, se, re, sf, rf,
):
    f32, bf16 = jnp.float32, jnp.bfloat16
    v = lax.axis_index("vocab")
    z = lax.axis_index("dp")
    core, chip = lax.rem(v, 2), v // 2
    chips = n_vocab // 2
    width, hidden_width = out_ref.shape
    half = hidden_width // 2
    span = half // split
    rows_a = width * span // LANES
    rows_b = rows_a // chips
    rows_c = rows_b // n_dp
    tile = min(256, span)
    partner = (chip * 2 + 1 - core, z)

    def in_plane(k):
        return (lax.rem(chip + k, chips) * 2 + core, z)

    def in_line(k):
        return (v, lax.rem(z + k, n_dp))

    def load(j):
        side = (1 - core) if j < split else core
        at = pl.ds(pl.multiple_of(side * half + (j % split) * span, LANES), span)
        return pltpu.make_async_copy(cot_ref.at[:, at], cot_buf.at[j], load_sem.at[j])

    for j in range(2 * split):
        load(j).start()
    barrier = pltpu.get_barrier_semaphore()
    peers = [partner] + [in_plane(k) for k in range(1, chips)] + [in_line(k) for k in range(1, n_dp)]
    for where in peers:
        pl.semaphore_signal(barrier, inc=1, device_id=where, device_id_type=MESH)
    emb_t[...] = emb_ref[...].T

    def product(j, target):
        def step(t, carry):
            at = pl.ds(pl.multiple_of(t * tile, tile), tile)
            y = jnp.dot(emb_t[...], cot_buf[j, :, at], preferred_element_type=f32)
            for b in range(tile // LANES):
                rows = pl.ds(pl.multiple_of((t * (tile // LANES) + b) * width, width), width)
                target[rows, :] = y[:, b * LANES : (b + 1) * LANES].astype(target.dtype)
            return carry

        lax.fori_loop(0, span // tile, step, 0)

    def copy_a(q):
        return remote(send_a.at[q], recv_a.at[q], sa.at[q], ra.at[q], partner)

    def copy_b(q, k):
        to = lax.rem(chip + k, chips)
        rows = pl.ds(pl.multiple_of(to * rows_b, rows_b), rows_b)
        return remote(
            send_b.at[q, rows, :], recv_b.at[q, k - 1], sb.at[q, k - 1], rb.at[q, k - 1], in_plane(k)
        )

    def copy_c(q, k):
        to = lax.rem(z + k, n_dp)
        rows = pl.ds(pl.multiple_of(to * rows_c, rows_c), rows_c)
        return remote(
            acc_b.at[q, rows, :], recv_c.at[q, k - 1], sc.at[q, k - 1], rc.at[q, k - 1], in_line(k)
        )

    def copy_d(q, k):
        rows = pl.ds(pl.multiple_of(chip * rows_b + z * rows_c, rows_c), rows_c)
        piece = full.at[core, q, rows, :]
        return remote(piece, piece, sd.at[q, k - 1], rd.at[q, k - 1], in_line(k))

    def copy_e(q, k):
        rows = pl.ds(pl.multiple_of(chip * rows_b, rows_b), rows_b)
        piece = full.at[core, q, rows, :]
        return remote(piece, piece, se.at[q, k - 1], re.at[q, k - 1], in_plane(k))

    def copy_f(q):
        piece = full.at[core, q]
        return remote(piece, piece, sf.at[q], rf.at[q], partner)

    for q in range(split):
        load(q).wait()
        product(q, send_a.at[q])
        if q == 0:
            pl.semaphore_wait(barrier, len(peers))
        copy_a(q).start()
    for q in range(split):
        load(split + q).wait()
        product(split + q, acc_a.at[q])
    plane = range(1, chips)
    line = range(1, n_dp)
    for q in range(split):
        copy_a(q).wait_recv()
        acc_a[q] = acc_a[q] + recv_a[q].astype(f32)
        send_b[q] = acc_a[q].astype(bf16)
        for k in plane:
            copy_b(q, k).start()
    for q in range(split):
        own = pl.ds(pl.multiple_of(chip * rows_b, rows_b), rows_b)
        total = acc_a[q, own, :]
        for k in plane:
            copy_b(q, k).wait_recv()
            total = total + recv_b[q, k - 1].astype(f32)
        acc_b[q] = total
        for k in line:
            copy_c(q, k).start()
    for q in range(split):
        own = pl.ds(pl.multiple_of(z * rows_c, rows_c), rows_c)
        total = acc_b[q, own, :]
        for k in line:
            copy_c(q, k).wait_recv()
            total = total + recv_c[q, k - 1]
        rows = pl.ds(pl.multiple_of(chip * rows_b + z * rows_c, rows_c), rows_c)
        full[core, q, rows, :] = (total * scaling).astype(bf16)
        for k in line:
            copy_d(q, k).start()
    for q in range(split):
        for k in line:
            copy_d(q, k).wait_recv()
        for k in plane:
            copy_e(q, k).start()
    for q in range(split):
        for k in plane:
            copy_e(q, k).wait_recv()
        copy_f(q).start()

    def unpack(side, q):
        for b in range(span // LANES):
            at = pl.ds(pl.multiple_of(side * half + q * span + b * LANES, LANES), LANES)
            out_ref[:, at] = full[side, q, pl.ds(b * width, width), :]

    for q in range(split):
        unpack(core, q)
    for q in range(split):
        copy_f(q).wait_recv()
        unpack(1 - core, q)
    for q in range(split):
        copy_a(q).wait_send()
        copy_f(q).wait_send()
        for k in plane:
            copy_b(q, k).wait_send()
            copy_e(q, k).wait_send()
        for k in line:
            copy_c(q, k).wait_send()
            copy_d(q, k).wait_send()


def reduce_terms(embedded, cotangent, scaling):
    n_vocab, n_dp = lax.axis_size("vocab"), lax.axis_size("dp")
    tokens, width = embedded.shape
    hidden_width = cotangent.shape[1]
    split = 2
    chips = n_vocab // 2
    span = hidden_width // (2 * split)
    rows_a = width * span // LANES
    rows_b = rows_a // chips
    rows_c = rows_b // n_dp
    f32, bf16 = jnp.float32, jnp.bfloat16
    dma = pltpu.SemaphoreType.DMA
    plane, line = max(1, chips - 1), max(1, n_dp - 1)
    return pl.pallas_call(
        functools.partial(reduce_kernel, n_vocab, n_dp, split, scaling),
        out_shape=jax.ShapeDtypeStruct((width, hidden_width), bf16),
        in_specs=[
            pl.BlockSpec(memory_space=pltpu.VMEM),
            pl.BlockSpec(memory_space=pl.ANY),
        ],
        out_specs=pl.BlockSpec(memory_space=pltpu.VMEM),
        scratch_shapes=[
            pltpu.VMEM((2 * split, tokens, span), bf16),
            pltpu.VMEM((width, tokens), bf16),
            pltpu.VMEM((split, rows_a, LANES), bf16),
            pltpu.VMEM((split, rows_a, LANES), bf16),
            pltpu.VMEM((split, rows_a, LANES), f32),
            pltpu.VMEM((split, rows_a, LANES), bf16),
            pltpu.VMEM((split, plane, rows_b, LANES), bf16),
            pltpu.VMEM((split, rows_b, LANES), f32),
            pltpu.VMEM((split, line, rows_c, LANES), f32),
            pltpu.VMEM((2, split, rows_a, LANES), bf16),
            dma((2 * split,)),
            dma((split,)), dma((split,)),
            dma((split, plane)), dma((split, plane)),
            dma((split, line)), dma((split, line)),
            dma((split, line)), dma((split, line)),
            dma((split, plane)), dma((split, plane)),
            dma((split,)), dma((split,)),
        ],
        compiler_params=pltpu.CompilerParams(collective_id=1, has_side_effects=True),
        name="reduce_terms",
    )(embedded, cotangent)


def body(token_ids, counts, table, projection, cotangent):
    tokens_here = token_ids.shape[0]
    held_rows = table.shape[0]
    width = table.shape[1]
    hidden_width = projection.shape[1]
    devices_all = lax.axis_size("vocab") * lax.axis_size("dp")
    capacity = max(4, 2 * tokens_here // devices_all)
    slots = devices_all * capacity
    bf16, f32 = jnp.bfloat16, jnp.float32

    owner = token_ids // held_rows
    local_row = token_ids - owner * held_rows
    hits = (owner[:, None] == jnp.arange(devices_all, dtype=jnp.int32)[None, :]).astype(bf16)
    order = jnp.arange(tokens_here, dtype=jnp.int32)
    before = (order[:, None] >= order[None, :]).astype(bf16)
    ranks = jnp.dot(before, hits, preferred_element_type=f32)
    rank = jnp.sum(ranks * hits.astype(f32), axis=1).astype(jnp.int32) - 1
    slot_index = jnp.where(order < counts[0], owner * capacity + rank, -1)
    place = (slot_index[:, None] == jnp.arange(slots, dtype=jnp.int32)[None, :]).astype(bf16)
    digits = jnp.stack(
        [local_row // 65536, (local_row // 256) % 256, local_row % 256, jnp.ones_like(local_row)]
    ).astype(bf16)
    found = jnp.dot(digits, place, preferred_element_type=f32).astype(jnp.int32)
    requests = found[0] * 65536 + found[1] * 256 + found[2] + found[3] - 1
    requests = jnp.where(found[3] > 0, requests, -1)

    received = exchange(requests.reshape(devices_all, capacity)).reshape(-1)
    valid = received >= 0
    safe_rows = jnp.maximum(received, 0)
    picked = jnp.where(valid[:, None], table[safe_rows], jnp.zeros((1, width), table.dtype))
    returned = exchange(picked.reshape(devices_all, capacity, width)).reshape(-1, width)

    token_grad = lax.dot_general(
        cotangent, projection, (((1,), (1,)), ((), ())), preferred_element_type=f32
    ).astype(bf16)
    outgoing = lax.dot_general(
        place, token_grad, (((0,), (0,)), ((), ())), preferred_element_type=f32
    ).astype(bf16)
    incoming = exchange(outgoing.reshape(devices_all, capacity, width)).reshape(-1, width)

    embedded = jnp.dot(place, returned, preferred_element_type=f32).astype(bf16)
    scaling = 1.0 / math.sqrt(tokens_here * devices_all)
    grad_projection = reduce_terms(embedded, cotangent, scaling).astype(f32)

    product = jnp.dot(embedded, projection, preferred_element_type=f32)
    hidden = product.astype(bf16)
    grad_table = scatter_rows(safe_rows, incoming.astype(f32), held_rows)
    return (hidden, grad_projection, grad_table)


def solution(mesh):
    return jax.shard_map(
        body,
        mesh=mesh,
        in_specs=(
            P(AXES),
            P(AXES),
            P(AXES, None),
            P(),
            P(AXES, None),
        ),
        out_specs=(P(AXES, None), P(), P(AXES, None)),
        check_vma=False,
    )
```

```python
import functools
import math

import jax
import jax.numpy as jnp
from jax import lax
from jax.experimental import pallas as pl
from jax.experimental.pallas import tpu as pltpu
from jax.sharding import PartitionSpec as P

AXES = ("vocab", "dp")
ACCS = 4


def exchange(blocks):
    return lax.all_to_all(blocks, AXES, split_axis=0, concat_axis=0, tiled=True)


def scatter_kernel(chunks, rows_ref, incoming_ref, out_ref, acc0, acc1, acc2, acc3, sems):
    accs = (acc0, acc1, acc2, acc3)
    held = acc0.shape[0]
    part = held // chunks
    count = incoming_ref.shape[0]

    def clear(i, carry):
        at = pl.ds(pl.multiple_of(i * 64, 64), 64)
        for acc in accs:
            acc[at, :] = jnp.zeros((64, acc.shape[1]), jnp.float32)
        return carry

    lax.fori_loop(0, held // 64, clear, 0)

    def add(i, carry):
        base = pl.multiple_of(i * 8, 8)
        block = incoming_ref[pl.ds(base, 8), :]
        for j in range(8):
            acc = accs[j % ACCS]
            at = pl.ds(rows_ref[base + j], 1)
            acc[at, :] = acc[at, :] + block[j : j + 1, :]
        return carry

    lax.fori_loop(0, count // 8, add, 0)

    def copy(c):
        at = pl.ds(c * part, part)
        return pltpu.make_async_copy(acc0.at[at, :], out_ref.at[at, :], sems.at[c])

    for c in range(chunks):

        def join(i, carry):
            at = pl.ds(pl.multiple_of(c * part + i * 64, 64), 64)
            acc0[at, :] = (acc0[at, :] + acc1[at, :]) + (acc2[at, :] + acc3[at, :])
            return carry

        lax.fori_loop(0, part // 64, join, 0)
        copy(c).start()
    for c in range(chunks):
        copy(c).wait()


def scatter_rows(rows, incoming, held_rows):
    width = incoming.shape[1]
    chunks = 4
    return pl.pallas_call(
        functools.partial(scatter_kernel, chunks),
        out_shape=jax.ShapeDtypeStruct((held_rows, width), jnp.float32),
        in_specs=[
            pl.BlockSpec(memory_space=pltpu.SMEM),
            pl.BlockSpec(memory_space=pltpu.VMEM),
        ],
        out_specs=pl.BlockSpec(memory_space=pl.ANY),
        scratch_shapes=[pltpu.VMEM((held_rows, width), jnp.float32)] * ACCS
        + [pltpu.SemaphoreType.DMA((chunks,))],
        cost_estimate=pl.CostEstimate(flops=0, bytes_accessed=12 << 20, transcendentals=0),
        name="scatter_rows",
    )(rows, incoming)

MESH = pl.DeviceIdType.MESH
LANES = 128


def remote(src, dst, send_sem, recv_sem, where):
    return pltpu.make_async_remote_copy(
        src_ref=src, dst_ref=dst, send_sem=send_sem, recv_sem=recv_sem,
        device_id=where, device_id_type=MESH,
    )


def reduce_kernel(
    n_vocab, n_dp, split, scaling,
    picked_ref, slot_row, slot_col, proj_ref, cot_ref, out_ref, emb_ref, incoming_ref,
    returned, outgoing, arrived, grad_sum, grad_half, rows_s, rows_r, grads_s, grads_r,
    cot_buf, emb_t, send_a, recv_a, acc_a, send_b, recv_b, acc_b, recv_c, full,
    load_sem, sa, ra, sb, rb, sc, rc, sd, rd, se, re, sf, rf,
):
    f32, bf16 = jnp.float32, jnp.bfloat16
    v = lax.axis_index("vocab")
    z = lax.axis_index("dp")
    core, chip = lax.rem(v, 2), v // 2
    chips = n_vocab // 2
    width, hidden_width = out_ref.shape
    half = hidden_width // 2
    span = half // split
    rows_a = width * span // LANES
    rows_b = rows_a // chips
    rows_c = rows_b // n_dp
    tile = min(256, span)
    partner = (chip * 2 + 1 - core, z)

    def in_plane(k):
        return (lax.rem(chip + k, chips) * 2 + core, z)

    def in_line(k):
        return (v, lax.rem(z + k, n_dp))

    def load(j):
        side = (1 - core) if j < split else core
        at = pl.ds(pl.multiple_of(side * half + (j % split) * span, LANES), span)
        return pltpu.make_async_copy(cot_ref.at[:, at], cot_buf.at[j], load_sem.at[j])

    for j in range(2 * split):
        load(j).start()
    devices_all = n_vocab * n_dp
    me = v * n_dp + z
    tokens = slot_row.shape[1]
    slots = returned.shape[0]
    capacity = slots // devices_all
    barrier = pltpu.get_barrier_semaphore()

    def device(k):
        to = lax.rem(me + k, devices_all)
        return to, (to // n_dp, lax.rem(to, n_dp))

    def greet(k, carry):
        pl.semaphore_signal(barrier, inc=1, device_id=device(k)[1], device_id_type=MESH)
        return carry

    def block(at):
        return pl.ds(pl.multiple_of(at * capacity, capacity), capacity)

    def copy_rows(k):
        to, where = device(k)
        return remote(
            picked_ref.at[block(to), :], returned.at[block(me), :], rows_s.at[k], rows_r.at[k], where
        )

    def copy_grads(k):
        to, where = device(k)
        return remote(
            outgoing.at[block(to), :], arrived.at[block(me), :], grads_s.at[k], grads_r.at[k], where
        )

    def each(action):
        def step(k, carry):
            action(k)
            return carry

        lax.fori_loop(1, devices_all, step, 0)

    lax.fori_loop(1, devices_all, greet, 0)
    pl.semaphore_wait(barrier, devices_all - 1)
    each(lambda k: copy_rows(k).start())
    returned[block(me), :] = picked_ref[block(me), :]

    rows_tile = min(256, tokens)
    for j in range(2 * split):
        load(j).wait()
        side = (1 - core) if j < split else core
        at = pl.ds(pl.multiple_of(side * half + (j % split) * span, LANES), span)

        def back(t, carry):
            rows = pl.ds(pl.multiple_of(t * rows_tile, rows_tile), rows_tile)
            y = lax.dot_general(
                cot_buf[j, rows, :], proj_ref[:, at], (((1,), (1,)), ((), ())),
                preferred_element_type=f32,
            )
            if j == 0:
                grad_sum[rows, :] = y
            else:
                grad_sum[rows, :] = grad_sum[rows, :] + y
            return carry

        lax.fori_loop(0, tokens // rows_tile, back, 0)
    grad_half[...] = grad_sum[...].astype(bf16)

    slot_tile = 256

    def spread(t, carry):
        base = pl.multiple_of(t * slot_tile, slot_tile)
        ids = lax.broadcasted_iota(jnp.int32, (slot_tile, tokens), 0) + base
        place = jnp.where(ids == slot_row[...], 1.0, 0.0).astype(bf16)
        y = jnp.dot(place, grad_half[...], preferred_element_type=f32)
        outgoing[pl.ds(base, slot_tile), :] = y.astype(bf16)
        return carry

    lax.fori_loop(0, slots // slot_tile, spread, 0)
    each(lambda k: copy_grads(k).start())
    arrived[block(me), :] = outgoing[block(me), :]
    each(lambda k: copy_rows(k).wait_recv())

    def embed(t, carry):
        rows = pl.ds(pl.multiple_of(t * rows_tile, rows_tile), rows_tile)
        ids = lax.broadcasted_iota(jnp.int32, (rows_tile, slots), 1)
        place = jnp.where(ids == slot_col[rows, :], 1.0, 0.0).astype(bf16)
        y = jnp.dot(place, returned[...], preferred_element_type=f32)
        emb_ref[rows, :] = y.astype(bf16)
        return carry

    lax.fori_loop(0, tokens // rows_tile, embed, 0)
    emb_t[...] = emb_ref[...].T

    def product(j, target):
        def step(t, carry):
            at = pl.ds(pl.multiple_of(t * tile, tile), tile)
            y = jnp.dot(emb_t[...], cot_buf[j, :, at], preferred_element_type=f32)
            for b in range(tile // LANES):
                rows = pl.ds(pl.multiple_of((t * (tile // LANES) + b) * width, width), width)
                target[rows, :] = y[:, b * LANES : (b + 1) * LANES].astype(target.dtype)
            return carry

        lax.fori_loop(0, span // tile, step, 0)

    def copy_a(q):
        return remote(send_a.at[q], recv_a.at[q], sa.at[q], ra.at[q], partner)

    def copy_b(q, k):
        to = lax.rem(chip + k, chips)
        rows = pl.ds(pl.multiple_of(to * rows_b, rows_b), rows_b)
        return remote(
            send_b.at[q, rows, :], recv_b.at[q, k - 1], sb.at[q, k - 1], rb.at[q, k - 1], in_plane(k)
        )

    def copy_c(q, k):
        to = lax.rem(z + k, n_dp)
        rows = pl.ds(pl.multiple_of(to * rows_c, rows_c), rows_c)
        return remote(
            acc_b.at[q, rows, :], recv_c.at[q, k - 1], sc.at[q, k - 1], rc.at[q, k - 1], in_line(k)
        )

    def copy_d(q, k):
        rows = pl.ds(pl.multiple_of(chip * rows_b + z * rows_c, rows_c), rows_c)
        piece = full.at[core, q, rows, :]
        return remote(piece, piece, sd.at[q, k - 1], rd.at[q, k - 1], in_line(k))

    def copy_e(q, k):
        rows = pl.ds(pl.multiple_of(chip * rows_b, rows_b), rows_b)
        piece = full.at[core, q, rows, :]
        return remote(piece, piece, se.at[q, k - 1], re.at[q, k - 1], in_plane(k))

    def copy_f(q):
        piece = full.at[core, q]
        return remote(piece, piece, sf.at[q], rf.at[q], partner)

    for q in range(split):
        product(q, send_a.at[q])
        copy_a(q).start()
    for q in range(split):
        product(split + q, acc_a.at[q])
    plane = range(1, chips)
    line = range(1, n_dp)
    for q in range(split):
        copy_a(q).wait_recv()
        acc_a[q] = acc_a[q] + recv_a[q].astype(f32)
        send_b[q] = acc_a[q].astype(bf16)
        for k in plane:
            copy_b(q, k).start()
    for q in range(split):
        own = pl.ds(pl.multiple_of(chip * rows_b, rows_b), rows_b)
        total = acc_a[q, own, :]
        for k in plane:
            copy_b(q, k).wait_recv()
            total = total + recv_b[q, k - 1].astype(f32)
        acc_b[q] = total
        for k in line:
            copy_c(q, k).start()
    for q in range(split):
        own = pl.ds(pl.multiple_of(z * rows_c, rows_c), rows_c)
        total = acc_b[q, own, :]
        for k in line:
            copy_c(q, k).wait_recv()
            total = total + recv_c[q, k - 1]
        rows = pl.ds(pl.multiple_of(chip * rows_b + z * rows_c, rows_c), rows_c)
        full[core, q, rows, :] = (total * scaling).astype(bf16)
        for k in line:
            copy_d(q, k).start()
    for q in range(split):
        for k in line:
            copy_d(q, k).wait_recv()
        for k in plane:
            copy_e(q, k).start()
    for q in range(split):
        for k in plane:
            copy_e(q, k).wait_recv()
        copy_f(q).start()

    def unpack(side, q):
        for b in range(span // LANES):
            at = pl.ds(pl.multiple_of(side * half + q * span + b * LANES, LANES), LANES)
            out_ref[:, at] = full[side, q, pl.ds(b * width, width), :]

    for q in range(split):
        unpack(core, q)
    for q in range(split):
        copy_f(q).wait_recv()
        unpack(1 - core, q)
    each(lambda k: copy_grads(k).wait_recv())
    incoming_ref[...] = arrived[...].astype(f32)
    each(lambda k: copy_rows(k).wait_send())
    each(lambda k: copy_grads(k).wait_send())
    for q in range(split):
        copy_a(q).wait_send()
        copy_f(q).wait_send()
        for k in plane:
            copy_b(q, k).wait_send()
            copy_e(q, k).wait_send()
        for k in line:
            copy_c(q, k).wait_send()
            copy_d(q, k).wait_send()


def reduce_terms(picked, slot_index, projection, cotangent, scaling):
    n_vocab, n_dp = lax.axis_size("vocab"), lax.axis_size("dp")
    tokens = slot_index.shape[0]
    slots, width = picked.shape
    devices_all = n_vocab * n_dp
    hidden_width = cotangent.shape[1]
    split = 2
    chips = n_vocab // 2
    span = hidden_width // (2 * split)
    rows_a = width * span // LANES
    rows_b = rows_a // chips
    rows_c = rows_b // n_dp
    f32, bf16 = jnp.float32, jnp.bfloat16
    dma = pltpu.SemaphoreType.DMA
    plane, line = max(1, chips - 1), max(1, n_dp - 1)
    return pl.pallas_call(
        functools.partial(reduce_kernel, n_vocab, n_dp, split, scaling),
        out_shape=[
            jax.ShapeDtypeStruct((width, hidden_width), bf16),
            jax.ShapeDtypeStruct((tokens, width), bf16),
            jax.ShapeDtypeStruct((slots, width), f32),
        ],
        in_specs=[pl.BlockSpec(memory_space=pltpu.VMEM)] * 4
        + [pl.BlockSpec(memory_space=pl.ANY)],
        out_specs=[pl.BlockSpec(memory_space=pltpu.VMEM)] * 3,
        scratch_shapes=[
            pltpu.VMEM((slots, width), bf16),
            pltpu.VMEM((slots, width), bf16),
            pltpu.VMEM((slots, width), bf16),
            pltpu.VMEM((tokens, width), f32),
            pltpu.VMEM((tokens, width), bf16),
            dma((devices_all,)), dma((devices_all,)),
            dma((devices_all,)), dma((devices_all,)),
            pltpu.VMEM((2 * split, tokens, span), bf16),
            pltpu.VMEM((width, tokens), bf16),
            pltpu.VMEM((split, rows_a, LANES), bf16),
            pltpu.VMEM((split, rows_a, LANES), bf16),
            pltpu.VMEM((split, rows_a, LANES), f32),
            pltpu.VMEM((split, rows_a, LANES), bf16),
            pltpu.VMEM((split, plane, rows_b, LANES), bf16),
            pltpu.VMEM((split, rows_b, LANES), f32),
            pltpu.VMEM((split, line, rows_c, LANES), f32),
            pltpu.VMEM((2, split, rows_a, LANES), bf16),
            dma((2 * split,)),
            dma((split,)), dma((split,)),
            dma((split, plane)), dma((split, plane)),
            dma((split, line)), dma((split, line)),
            dma((split, line)), dma((split, line)),
            dma((split, plane)), dma((split, plane)),
            dma((split,)), dma((split,)),
        ],
        compiler_params=pltpu.CompilerParams(collective_id=1, has_side_effects=True),
        name="reduce_terms",
    )(picked, slot_index[None, :], slot_index[:, None], projection, cotangent)


def body(token_ids, counts, table, projection, cotangent):
    tokens_here = token_ids.shape[0]
    held_rows = table.shape[0]
    width = table.shape[1]
    hidden_width = projection.shape[1]
    devices_all = lax.axis_size("vocab") * lax.axis_size("dp")
    capacity = max(4, 2 * tokens_here // devices_all)
    slots = devices_all * capacity
    bf16, f32 = jnp.bfloat16, jnp.float32

    owner = token_ids // held_rows
    local_row = token_ids - owner * held_rows
    hits = (owner[:, None] == jnp.arange(devices_all, dtype=jnp.int32)[None, :]).astype(bf16)
    order = jnp.arange(tokens_here, dtype=jnp.int32)
    before = (order[:, None] >= order[None, :]).astype(bf16)
    ranks = jnp.dot(before, hits, preferred_element_type=f32)
    rank = jnp.sum(ranks * hits.astype(f32), axis=1).astype(jnp.int32) - 1
    slot_index = jnp.where(order < counts[0], owner * capacity + rank, -1)
    place = (slot_index[:, None] == jnp.arange(slots, dtype=jnp.int32)[None, :]).astype(bf16)
    digits = jnp.stack(
        [local_row // 65536, (local_row // 256) % 256, local_row % 256, jnp.ones_like(local_row)]
    ).astype(bf16)
    found = jnp.dot(digits, place, preferred_element_type=f32).astype(jnp.int32)
    requests = found[0] * 65536 + found[1] * 256 + found[2] + found[3] - 1
    requests = jnp.where(found[3] > 0, requests, -1)

    received = exchange(requests.reshape(devices_all, capacity)).reshape(-1)
    safe_rows = jnp.maximum(received, 0)
    scaling = 1.0 / math.sqrt(tokens_here * devices_all)
    terms, embedded, incoming = reduce_terms(
        table[safe_rows], slot_index, projection, cotangent, scaling
    )
    grad_projection = terms.astype(f32)

    product = jnp.dot(embedded, projection, preferred_element_type=f32)
    hidden = product.astype(bf16)
    grad_table = scatter_rows(safe_rows, incoming, held_rows)
    return (hidden, grad_projection, grad_table)


def solution(mesh):
    return jax.shard_map(
        body,
        mesh=mesh,
        in_specs=(
            P(AXES),
            P(AXES),
            P(AXES, None),
            P(),
            P(AXES, None),
        ),
        out_specs=(P(AXES, None), P(), P(AXES, None)),
        check_vma=False,
    )
```

```python
import functools
import math

import jax
import jax.numpy as jnp
from jax import lax
from jax.experimental import pallas as pl
from jax.experimental.pallas import tpu as pltpu
from jax.sharding import PartitionSpec as P

AXES = ("vocab", "dp")
ACCS = 4


def scatter_kernel(chunks, rows_ref, incoming_ref, out_ref, acc0, acc1, acc2, acc3, sems):
    accs = (acc0, acc1, acc2, acc3)
    held = acc0.shape[0]
    part = held // chunks
    count = incoming_ref.shape[0]

    def clear(i, carry):
        at = pl.ds(pl.multiple_of(i * 64, 64), 64)
        for acc in accs:
            acc[at, :] = jnp.zeros((64, acc.shape[1]), jnp.float32)
        return carry

    lax.fori_loop(0, held // 64, clear, 0)

    def add(i, carry):
        base = pl.multiple_of(i * 8, 8)
        block = incoming_ref[pl.ds(base, 8), :]
        for j in range(8):
            acc = accs[j % ACCS]
            at = pl.ds(rows_ref[base + j], 1)
            acc[at, :] = acc[at, :] + block[j : j + 1, :]
        return carry

    lax.fori_loop(0, count // 8, add, 0)

    def copy(c):
        at = pl.ds(c * part, part)
        return pltpu.make_async_copy(acc0.at[at, :], out_ref.at[at, :], sems.at[c])

    for c in range(chunks):

        def join(i, carry):
            at = pl.ds(pl.multiple_of(c * part + i * 64, 64), 64)
            acc0[at, :] = (acc0[at, :] + acc1[at, :]) + (acc2[at, :] + acc3[at, :])
            return carry

        lax.fori_loop(0, part // 64, join, 0)
        copy(c).start()
    for c in range(chunks):
        copy(c).wait()


def scatter_rows(rows, incoming, held_rows):
    width = incoming.shape[1]
    chunks = 4
    return pl.pallas_call(
        functools.partial(scatter_kernel, chunks),
        out_shape=jax.ShapeDtypeStruct((held_rows, width), jnp.float32),
        in_specs=[
            pl.BlockSpec(memory_space=pltpu.SMEM),
            pl.BlockSpec(memory_space=pltpu.VMEM),
        ],
        out_specs=pl.BlockSpec(memory_space=pl.ANY),
        scratch_shapes=[pltpu.VMEM((held_rows, width), jnp.float32)] * ACCS
        + [pltpu.SemaphoreType.DMA((chunks,))],
        cost_estimate=pl.CostEstimate(flops=0, bytes_accessed=12 << 20, transcendentals=0),
        name="scatter_rows",
    )(rows, incoming)

MESH = pl.DeviceIdType.MESH
LANES = 128


def remote(src, dst, send_sem, recv_sem, where):
    return pltpu.make_async_remote_copy(
        src_ref=src, dst_ref=dst, send_sem=send_sem, recv_sem=recv_sem,
        device_id=where, device_id_type=MESH,
    )


def reduce_kernel(
    n_vocab, n_dp, split, scaling,
    asked_ref, slot_row, slot_col, proj_ref, cot_ref, table_ref,
    out_ref, emb_ref, incoming_ref, wanted_ref,
    wanted, wanted_s, table_half, table_full, stage, picked, table_sem, want_sem, asks_s, asks_r,
    returned, outgoing, arrived, grad_sum, grad_half, rows_s, rows_r, grads_s, grads_r,
    cot_buf, emb_t, send_a, recv_a, acc_a, send_b, recv_b, acc_b, recv_c, full,
    load_sem, sa, ra, sb, rb, sc, rc, sd, rd, se, re, sf, rf,
):
    f32, bf16 = jnp.float32, jnp.bfloat16
    v = lax.axis_index("vocab")
    z = lax.axis_index("dp")
    core, chip = lax.rem(v, 2), v // 2
    chips = n_vocab // 2
    width, hidden_width = out_ref.shape
    half = hidden_width // 2
    span = half // split
    rows_a = width * span // LANES
    rows_b = rows_a // chips
    rows_c = rows_b // n_dp
    tile = min(256, span)
    partner = (chip * 2 + 1 - core, z)

    def in_plane(k):
        return (lax.rem(chip + k, chips) * 2 + core, z)

    def in_line(k):
        return (v, lax.rem(z + k, n_dp))

    def load(j):
        side = (1 - core) if j < split else core
        at = pl.ds(pl.multiple_of(side * half + (j % split) * span, LANES), span)
        return pltpu.make_async_copy(cot_ref.at[:, at], cot_buf.at[j], load_sem.at[j])

    table_load = pltpu.make_async_copy(table_ref, table_half, table_sem)
    table_load.start()
    for j in range(2 * split):
        load(j).start()
    devices_all = n_vocab * n_dp
    me = v * n_dp + z
    tokens = slot_row.shape[1]
    slots = returned.shape[0]
    capacity = slots // devices_all
    barrier = pltpu.get_barrier_semaphore()

    def device(k):
        to = lax.rem(me + k, devices_all)
        return to, (to // n_dp, lax.rem(to, n_dp))

    def greet(k, carry):
        pl.semaphore_signal(barrier, inc=1, device_id=device(k)[1], device_id_type=MESH)
        return carry

    def block(at):
        return pl.ds(pl.multiple_of(at * capacity, capacity), capacity)

    def copy_asks(k):
        to, where = device(k)
        return remote(asked_ref.at[to], wanted.at[me], asks_s.at[k], asks_r.at[k], where)

    def copy_rows(k):
        to, where = device(k)
        return remote(
            picked.at[block(to), :], returned.at[block(me), :], rows_s.at[k], rows_r.at[k], where
        )

    def copy_grads(k):
        to, where = device(k)
        return remote(
            outgoing.at[block(to), :], arrived.at[block(me), :], grads_s.at[k], grads_r.at[k], where
        )

    def each(action):
        def step(k, carry):
            action(k)
            return carry

        lax.fori_loop(1, devices_all, step, 0)

    lax.fori_loop(1, devices_all, greet, 0)
    pl.semaphore_wait(barrier, devices_all - 1)
    each(lambda k: copy_asks(k).start())
    wanted[me] = asked_ref[me]
    table_load.wait()
    held_rows = table_half.shape[0]
    wide = min(256, held_rows)

    def widen(i, carry):
        rows = pl.ds(pl.multiple_of(i * wide, wide), wide)
        table_full[rows, :] = table_half[rows, :].astype(f32)
        return carry

    lax.fori_loop(0, held_rows // wide, widen, 0)
    each(lambda k: copy_asks(k).wait_recv())
    to_scalars = pltpu.make_async_copy(wanted, wanted_s, want_sem)
    to_scalars.start()
    to_scalars.wait()

    def pick(at):
        for i in range(capacity):
            row = jnp.maximum(wanted_s[at, 0, i], 0)
            stage[i : i + 1, :] = table_full[pl.ds(row, 1), :]
        return stage[...].astype(bf16)

    def serve(k):
        at = device(k)[0]
        picked[block(at), :] = pick(at)
        copy_rows(k).start()

    each(serve)
    returned[block(me), :] = pick(me)
    wanted_ref[...] = wanted[...]

    rows_tile = min(256, tokens)
    for j in range(2 * split):
        load(j).wait()
        side = (1 - core) if j < split else core
        at = pl.ds(pl.multiple_of(side * half + (j % split) * span, LANES), span)

        def back(t, carry):
            rows = pl.ds(pl.multiple_of(t * rows_tile, rows_tile), rows_tile)
            y = lax.dot_general(
                cot_buf[j, rows, :], proj_ref[:, at], (((1,), (1,)), ((), ())),
                preferred_element_type=f32,
            )
            if j == 0:
                grad_sum[rows, :] = y
            else:
                grad_sum[rows, :] = grad_sum[rows, :] + y
            return carry

        lax.fori_loop(0, tokens // rows_tile, back, 0)
    grad_half[...] = grad_sum[...].astype(bf16)

    slot_tile = 256

    def spread(t, carry):
        base = pl.multiple_of(t * slot_tile, slot_tile)
        ids = lax.broadcasted_iota(jnp.int32, (slot_tile, tokens), 0) + base
        place = jnp.where(ids == slot_row[...], 1.0, 0.0).astype(bf16)
        y = jnp.dot(place, grad_half[...], preferred_element_type=f32)
        outgoing[pl.ds(base, slot_tile), :] = y.astype(bf16)
        return carry

    lax.fori_loop(0, slots // slot_tile, spread, 0)
    each(lambda k: copy_grads(k).start())
    arrived[block(me), :] = outgoing[block(me), :]
    each(lambda k: copy_rows(k).wait_recv())

    def embed(t, carry):
        rows = pl.ds(pl.multiple_of(t * rows_tile, rows_tile), rows_tile)
        ids = lax.broadcasted_iota(jnp.int32, (rows_tile, slots), 1)
        place = jnp.where(ids == slot_col[rows, :], 1.0, 0.0).astype(bf16)
        y = jnp.dot(place, returned[...], preferred_element_type=f32)
        emb_ref[rows, :] = y.astype(bf16)
        return carry

    lax.fori_loop(0, tokens // rows_tile, embed, 0)
    emb_t[...] = emb_ref[...].T

    def product(j, target):
        def step(t, carry):
            at = pl.ds(pl.multiple_of(t * tile, tile), tile)
            y = jnp.dot(emb_t[...], cot_buf[j, :, at], preferred_element_type=f32)
            for b in range(tile // LANES):
                rows = pl.ds(pl.multiple_of((t * (tile // LANES) + b) * width, width), width)
                target[rows, :] = y[:, b * LANES : (b + 1) * LANES].astype(target.dtype)
            return carry

        lax.fori_loop(0, span // tile, step, 0)

    def copy_a(q):
        return remote(send_a.at[q], recv_a.at[q], sa.at[q], ra.at[q], partner)

    def copy_b(q, k):
        to = lax.rem(chip + k, chips)
        rows = pl.ds(pl.multiple_of(to * rows_b, rows_b), rows_b)
        return remote(
            send_b.at[q, rows, :], recv_b.at[q, k - 1], sb.at[q, k - 1], rb.at[q, k - 1], in_plane(k)
        )

    def copy_c(q, k):
        to = lax.rem(z + k, n_dp)
        rows = pl.ds(pl.multiple_of(to * rows_c, rows_c), rows_c)
        return remote(
            acc_b.at[q, rows, :], recv_c.at[q, k - 1], sc.at[q, k - 1], rc.at[q, k - 1], in_line(k)
        )

    def copy_d(q, k):
        rows = pl.ds(pl.multiple_of(chip * rows_b + z * rows_c, rows_c), rows_c)
        piece = full.at[core, q, rows, :]
        return remote(piece, piece, sd.at[q, k - 1], rd.at[q, k - 1], in_line(k))

    def copy_e(q, k):
        rows = pl.ds(pl.multiple_of(chip * rows_b, rows_b), rows_b)
        piece = full.at[core, q, rows, :]
        return remote(piece, piece, se.at[q, k - 1], re.at[q, k - 1], in_plane(k))

    def copy_f(q):
        piece = full.at[core, q]
        return remote(piece, piece, sf.at[q], rf.at[q], partner)

    for q in range(split):
        product(q, send_a.at[q])
        copy_a(q).start()
    for q in range(split):
        product(split + q, acc_a.at[q])
    plane = range(1, chips)
    line = range(1, n_dp)
    for q in range(split):
        copy_a(q).wait_recv()
        acc_a[q] = acc_a[q] + recv_a[q].astype(f32)
        send_b[q] = acc_a[q].astype(bf16)
        for k in plane:
            copy_b(q, k).start()
    for q in range(split):
        own = pl.ds(pl.multiple_of(chip * rows_b, rows_b), rows_b)
        total = acc_a[q, own, :]
        for k in plane:
            copy_b(q, k).wait_recv()
            total = total + recv_b[q, k - 1].astype(f32)
        acc_b[q] = total
        for k in line:
            copy_c(q, k).start()
    for q in range(split):
        own = pl.ds(pl.multiple_of(z * rows_c, rows_c), rows_c)
        total = acc_b[q, own, :]
        for k in line:
            copy_c(q, k).wait_recv()
            total = total + recv_c[q, k - 1]
        rows = pl.ds(pl.multiple_of(chip * rows_b + z * rows_c, rows_c), rows_c)
        full[core, q, rows, :] = (total * scaling).astype(bf16)
        for k in line:
            copy_d(q, k).start()
    for q in range(split):
        for k in line:
            copy_d(q, k).wait_recv()
        for k in plane:
            copy_e(q, k).start()
    for q in range(split):
        for k in plane:
            copy_e(q, k).wait_recv()
        copy_f(q).start()

    def unpack(side, q):
        for b in range(span // LANES):
            at = pl.ds(pl.multiple_of(side * half + q * span + b * LANES, LANES), LANES)
            out_ref[:, at] = full[side, q, pl.ds(b * width, width), :]

    for q in range(split):
        unpack(core, q)
    for q in range(split):
        copy_f(q).wait_recv()
        unpack(1 - core, q)
    each(lambda k: copy_grads(k).wait_recv())
    incoming_ref[...] = arrived[...].astype(f32)
    each(lambda k: copy_asks(k).wait_send())
    each(lambda k: copy_rows(k).wait_send())
    each(lambda k: copy_grads(k).wait_send())
    for q in range(split):
        copy_a(q).wait_send()
        copy_f(q).wait_send()
        for k in plane:
            copy_b(q, k).wait_send()
            copy_e(q, k).wait_send()
        for k in line:
            copy_c(q, k).wait_send()
            copy_d(q, k).wait_send()


def reduce_terms(asked, slot_index, projection, cotangent, table, capacity, scaling):
    n_vocab, n_dp = lax.axis_size("vocab"), lax.axis_size("dp")
    tokens = slot_index.shape[0]
    held_rows, width = table.shape
    devices_all = n_vocab * n_dp
    slots = devices_all * capacity
    hidden_width = cotangent.shape[1]
    split = 2
    chips = n_vocab // 2
    span = hidden_width // (2 * split)
    rows_a = width * span // LANES
    rows_b = rows_a // chips
    rows_c = rows_b // n_dp
    f32, bf16 = jnp.float32, jnp.bfloat16
    dma = pltpu.SemaphoreType.DMA
    plane, line = max(1, chips - 1), max(1, n_dp - 1)
    return pl.pallas_call(
        functools.partial(reduce_kernel, n_vocab, n_dp, split, scaling),
        out_shape=[
            jax.ShapeDtypeStruct((width, hidden_width), bf16),
            jax.ShapeDtypeStruct((tokens, width), bf16),
            jax.ShapeDtypeStruct((slots, width), f32),
            jax.ShapeDtypeStruct(asked.shape, jnp.int32),
        ],
        in_specs=[pl.BlockSpec(memory_space=pltpu.VMEM)] * 4
        + [pl.BlockSpec(memory_space=pl.ANY)] * 2,
        out_specs=[pl.BlockSpec(memory_space=pltpu.VMEM)] * 4,
        scratch_shapes=[
            pltpu.VMEM(asked.shape, jnp.int32),
            pltpu.SMEM(asked.shape, jnp.int32),
            pltpu.VMEM((held_rows, width), bf16),
            pltpu.VMEM((held_rows, width), f32),
            pltpu.VMEM((capacity, width), f32),
            pltpu.VMEM((slots, width), bf16),
            dma, dma,
            dma((devices_all,)), dma((devices_all,)),
            pltpu.VMEM((slots, width), bf16),
            pltpu.VMEM((slots, width), bf16),
            pltpu.VMEM((slots, width), bf16),
            pltpu.VMEM((tokens, width), f32),
            pltpu.VMEM((tokens, width), bf16),
            dma((devices_all,)), dma((devices_all,)),
            dma((devices_all,)), dma((devices_all,)),
            pltpu.VMEM((2 * split, tokens, span), bf16),
            pltpu.VMEM((width, tokens), bf16),
            pltpu.VMEM((split, rows_a, LANES), bf16),
            pltpu.VMEM((split, rows_a, LANES), bf16),
            pltpu.VMEM((split, rows_a, LANES), f32),
            pltpu.VMEM((split, rows_a, LANES), bf16),
            pltpu.VMEM((split, plane, rows_b, LANES), bf16),
            pltpu.VMEM((split, rows_b, LANES), f32),
            pltpu.VMEM((split, line, rows_c, LANES), f32),
            pltpu.VMEM((2, split, rows_a, LANES), bf16),
            dma((2 * split,)),
            dma((split,)), dma((split,)),
            dma((split, plane)), dma((split, plane)),
            dma((split, line)), dma((split, line)),
            dma((split, line)), dma((split, line)),
            dma((split, plane)), dma((split, plane)),
            dma((split,)), dma((split,)),
        ],
        compiler_params=pltpu.CompilerParams(collective_id=1, has_side_effects=True),
        name="reduce_terms",
    )(asked, slot_index[None, :], slot_index[:, None], projection, cotangent, table)


def body(token_ids, counts, table, projection, cotangent):
    tokens_here = token_ids.shape[0]
    held_rows = table.shape[0]
    width = table.shape[1]
    hidden_width = projection.shape[1]
    devices_all = lax.axis_size("vocab") * lax.axis_size("dp")
    capacity = max(4, 2 * tokens_here // devices_all)
    slots = devices_all * capacity
    bf16, f32 = jnp.bfloat16, jnp.float32

    owner = token_ids // held_rows
    local_row = token_ids - owner * held_rows
    hits = (owner[:, None] == jnp.arange(devices_all, dtype=jnp.int32)[None, :]).astype(bf16)
    order = jnp.arange(tokens_here, dtype=jnp.int32)
    before = (order[:, None] >= order[None, :]).astype(bf16)
    ranks = jnp.dot(before, hits, preferred_element_type=f32)
    rank = jnp.sum(ranks * hits.astype(f32), axis=1).astype(jnp.int32) - 1
    slot_index = jnp.where(order < counts[0], owner * capacity + rank, -1)
    place = (slot_index[:, None] == jnp.arange(slots, dtype=jnp.int32)[None, :]).astype(bf16)
    digits = jnp.stack(
        [local_row // 65536, (local_row // 256) % 256, local_row % 256, jnp.ones_like(local_row)]
    ).astype(bf16)
    found = jnp.dot(digits, place, preferred_element_type=f32).astype(jnp.int32)
    requests = found[0] * 65536 + found[1] * 256 + found[2] + found[3] - 1
    requests = jnp.where(found[3] > 0, requests, -1)

    asked = jnp.pad(
        requests.reshape(devices_all, 1, capacity),
        ((0, 0), (0, 0), (0, -capacity % LANES)),
        constant_values=-1,
    )
    scaling = 1.0 / math.sqrt(tokens_here * devices_all)
    terms, embedded, incoming, wanted = reduce_terms(
        asked, slot_index, projection, cotangent, table, capacity, scaling
    )
    safe_rows = jnp.maximum(wanted[:, 0, :capacity].reshape(-1), 0)
    grad_projection = terms.astype(f32)

    product = jnp.dot(embedded, projection, preferred_element_type=f32)
    hidden = product.astype(bf16)
    grad_table = scatter_rows(safe_rows, incoming, held_rows)
    return (hidden, grad_projection, grad_table)


def solution(mesh):
    return jax.shard_map(
        body,
        mesh=mesh,
        in_specs=(
            P(AXES),
            P(AXES),
            P(AXES, None),
            P(),
            P(AXES, None),
        ),
        out_specs=(P(AXES, None), P(), P(AXES, None)),
        check_vma=False,
    )
```

```python
import functools
import math

import jax
import jax.numpy as jnp
from jax import lax
from jax.experimental import pallas as pl
from jax.experimental.pallas import tpu as pltpu
from jax.sharding import PartitionSpec as P

AXES = ("vocab", "dp")
ACCS = 4


def finish_kernel(
    capacity, chunks, wanted_ref, incoming_ref, emb_ref, proj_ref, terms_ref,
    table_out, hidden_out, proj_out,
    acc0, acc1, acc2, acc3, hid, grad, table_sems, hidden_sems, proj_sem,
):
    f32, bf16 = jnp.float32, jnp.bfloat16
    accs = (acc0, acc1, acc2, acc3)
    held, width = acc0.shape
    part = held // chunks
    slots = incoming_ref.shape[0]
    tokens, hidden_width = hid.shape
    high, wide = min(256, tokens), min(256, hidden_width)
    blocks, tiles = tokens // high, hidden_width // wide
    per = slots // (blocks * tiles)
    group = min(8, per, capacity)

    def convert(i, carry):
        at = pl.ds(pl.multiple_of(i * wide, wide), wide)
        grad[:, at] = terms_ref[:, at].astype(f32)
        return carry

    lax.fori_loop(0, tiles, convert, 0)
    proj_copy = pltpu.make_async_copy(grad, proj_out, proj_sem)
    proj_copy.start()

    def clear(i, carry):
        at = pl.ds(pl.multiple_of(i * 64, 64), 64)
        for acc in accs:
            acc[at, :] = jnp.zeros((64, width), f32)
        return carry

    lax.fori_loop(0, held // 64, clear, 0)

    def hidden_copy(r):
        at = pl.ds(r * high, high)
        return pltpu.make_async_copy(hid.at[at, :], hidden_out.at[at, :], hidden_sems.at[r])

    for r in range(blocks):

        def step(t, carry):
            at = pl.ds(pl.multiple_of(t * wide, wide), wide)
            y = jnp.dot(emb_ref[r * high : (r + 1) * high, :], proj_ref[:, at], preferred_element_type=f32)
            start = (r * tiles + t) * per
            for g in range(per // group):
                base = pl.multiple_of(start + g * group, group)
                block = incoming_ref[pl.ds(base, group), :]
                source = base // capacity
                first = lax.rem(base, capacity)
                for j in range(group):
                    acc = accs[j % ACCS]
                    row = pl.ds(jnp.maximum(wanted_ref[source, 0, first + j], 0), 1)
                    acc[row, :] = acc[row, :] + block[j : j + 1, :]
            hid[r * high : (r + 1) * high, at] = y.astype(bf16)
            return carry

        lax.fori_loop(0, tiles, step, 0)
        hidden_copy(r).start()

    def table_copy(c):
        at = pl.ds(c * part, part)
        return pltpu.make_async_copy(acc0.at[at, :], table_out.at[at, :], table_sems.at[c])

    for c in range(chunks):

        def join(i, carry):
            at = pl.ds(pl.multiple_of(c * part + i * 64, 64), 64)
            acc0[at, :] = (acc0[at, :] + acc1[at, :]) + (acc2[at, :] + acc3[at, :])
            return carry

        lax.fori_loop(0, part // 64, join, 0)
        table_copy(c).start()
    proj_copy.wait()
    for r in range(blocks):
        hidden_copy(r).wait()
    for c in range(chunks):
        table_copy(c).wait()


def finish(wanted, incoming, embedded, projection, terms, held_rows, capacity):
    tokens, width = embedded.shape
    hidden_width = projection.shape[1]
    chunks = 8
    f32, bf16 = jnp.float32, jnp.bfloat16
    dma = pltpu.SemaphoreType.DMA
    return pl.pallas_call(
        functools.partial(finish_kernel, capacity, chunks),
        out_shape=[
            jax.ShapeDtypeStruct((held_rows, width), f32),
            jax.ShapeDtypeStruct((tokens, hidden_width), bf16),
            jax.ShapeDtypeStruct((width, hidden_width), f32),
        ],
        in_specs=[pl.BlockSpec(memory_space=pltpu.SMEM)]
        + [pl.BlockSpec(memory_space=pltpu.VMEM)] * 4,
        out_specs=[pl.BlockSpec(memory_space=pl.ANY)] * 3,
        scratch_shapes=[pltpu.VMEM((held_rows, width), f32)] * ACCS
        + [
            pltpu.VMEM((tokens, hidden_width), bf16),
            pltpu.VMEM((width, hidden_width), f32),
            dma((chunks,)),
            dma((tokens // min(256, tokens),)),
            dma,
        ],
        name="finish",
    )(wanted, incoming, embedded, projection, terms)


MESH = pl.DeviceIdType.MESH
LANES = 128


def remote(src, dst, send_sem, recv_sem, where):
    return pltpu.make_async_remote_copy(
        src_ref=src, dst_ref=dst, send_sem=send_sem, recv_sem=recv_sem,
        device_id=where, device_id_type=MESH,
    )


def reduce_kernel(
    n_vocab, n_dp, split, scaling,
    asked_ref, slot_row, slot_col, proj_ref, cot_ref, table_ref,
    out_ref, emb_ref, incoming_ref, wanted_ref,
    wanted, wanted_s, table_half, table_full, stage, picked, table_sem, want_sem, asks_s, asks_r,
    returned, outgoing, arrived, grad_sum, grad_half, rows_s, rows_r, grads_s, grads_r,
    cot_buf, emb_t, send_a, recv_a, acc_a, send_b, recv_b, acc_b, recv_c, full,
    load_sem, sa, ra, sb, rb, sc, rc, sd, rd, se, re, sf, rf,
):
    f32, bf16 = jnp.float32, jnp.bfloat16
    v = lax.axis_index("vocab")
    z = lax.axis_index("dp")
    core, chip = lax.rem(v, 2), v // 2
    chips = n_vocab // 2
    width, hidden_width = out_ref.shape
    half = hidden_width // 2
    span = half // split
    rows_a = width * span // LANES
    rows_b = rows_a // chips
    rows_c = rows_b // n_dp
    tile = min(256, span)
    partner = (chip * 2 + 1 - core, z)

    def in_plane(k):
        return (lax.rem(chip + k, chips) * 2 + core, z)

    def in_line(k):
        return (v, lax.rem(z + k, n_dp))

    def load(j):
        side = (1 - core) if j < split else core
        at = pl.ds(pl.multiple_of(side * half + (j % split) * span, LANES), span)
        return pltpu.make_async_copy(cot_ref.at[:, at], cot_buf.at[j], load_sem.at[j])

    table_load = pltpu.make_async_copy(table_ref, table_half, table_sem)
    table_load.start()
    for j in range(2 * split):
        load(j).start()
    devices_all = n_vocab * n_dp
    me = v * n_dp + z
    tokens = slot_row.shape[1]
    slots = returned.shape[0]
    capacity = slots // devices_all
    barrier = pltpu.get_barrier_semaphore()

    def device(k):
        to = lax.rem(me + k, devices_all)
        return to, (to // n_dp, lax.rem(to, n_dp))

    def greet(k, carry):
        pl.semaphore_signal(barrier, inc=1, device_id=device(k)[1], device_id_type=MESH)
        return carry

    def block(at):
        return pl.ds(pl.multiple_of(at * capacity, capacity), capacity)

    def copy_asks(k):
        to, where = device(k)
        return remote(asked_ref.at[to], wanted.at[me], asks_s.at[k], asks_r.at[k], where)

    def copy_rows(k):
        to, where = device(k)
        return remote(
            picked.at[block(to), :], returned.at[block(me), :], rows_s.at[k], rows_r.at[k], where
        )

    def copy_grads(k):
        to, where = device(k)
        return remote(
            outgoing.at[block(to), :], arrived.at[block(me), :], grads_s.at[k], grads_r.at[k], where
        )

    def each(action):
        def step(k, carry):
            action(k)
            return carry

        lax.fori_loop(1, devices_all, step, 0)

    lax.fori_loop(1, devices_all, greet, 0)
    pl.semaphore_wait(barrier, devices_all - 1)
    each(lambda k: copy_asks(k).start())
    wanted[me] = asked_ref[me]
    table_load.wait()
    held_rows = table_half.shape[0]
    wide = min(256, held_rows)

    def widen(i, carry):
        rows = pl.ds(pl.multiple_of(i * wide, wide), wide)
        table_full[rows, :] = table_half[rows, :].astype(f32)
        return carry

    lax.fori_loop(0, held_rows // wide, widen, 0)
    each(lambda k: copy_asks(k).wait_recv())
    to_scalars = pltpu.make_async_copy(wanted, wanted_s, want_sem)
    to_scalars.start()
    to_scalars.wait()

    def pick(at):
        for i in range(capacity):
            row = jnp.maximum(wanted_s[at, 0, i], 0)
            stage[i : i + 1, :] = table_full[pl.ds(row, 1), :]
        return stage[...].astype(bf16)

    def serve(k):
        at = device(k)[0]
        picked[block(at), :] = pick(at)
        copy_rows(k).start()

    each(serve)
    returned[block(me), :] = pick(me)
    wanted_ref[...] = wanted[...]

    rows_tile = min(256, tokens)
    for j in range(2 * split):
        load(j).wait()
        side = (1 - core) if j < split else core
        at = pl.ds(pl.multiple_of(side * half + (j % split) * span, LANES), span)

        def back(t, carry):
            rows = pl.ds(pl.multiple_of(t * rows_tile, rows_tile), rows_tile)
            y = lax.dot_general(
                cot_buf[j, rows, :], proj_ref[:, at], (((1,), (1,)), ((), ())),
                preferred_element_type=f32,
            )
            if j == 0:
                grad_sum[rows, :] = y
            else:
                grad_sum[rows, :] = grad_sum[rows, :] + y
            return carry

        lax.fori_loop(0, tokens // rows_tile, back, 0)
    grad_half[...] = grad_sum[...].astype(bf16)

    slot_tile = 256

    def spread(t, carry):
        base = pl.multiple_of(t * slot_tile, slot_tile)
        ids = lax.broadcasted_iota(jnp.int32, (slot_tile, tokens), 0) + base
        place = jnp.where(ids == slot_row[...], 1.0, 0.0).astype(bf16)
        y = jnp.dot(place, grad_half[...], preferred_element_type=f32)
        outgoing[pl.ds(base, slot_tile), :] = y.astype(bf16)
        return carry

    lax.fori_loop(0, slots // slot_tile, spread, 0)
    each(lambda k: copy_grads(k).start())
    arrived[block(me), :] = outgoing[block(me), :]
    each(lambda k: copy_rows(k).wait_recv())

    def embed(t, carry):
        rows = pl.ds(pl.multiple_of(t * rows_tile, rows_tile), rows_tile)
        ids = lax.broadcasted_iota(jnp.int32, (rows_tile, slots), 1)
        place = jnp.where(ids == slot_col[rows, :], 1.0, 0.0).astype(bf16)
        y = jnp.dot(place, returned[...], preferred_element_type=f32)
        emb_ref[rows, :] = y.astype(bf16)
        return carry

    lax.fori_loop(0, tokens // rows_tile, embed, 0)
    emb_t[...] = emb_ref[...].T

    def product(j, target):
        def step(t, carry):
            at = pl.ds(pl.multiple_of(t * tile, tile), tile)
            y = jnp.dot(emb_t[...], cot_buf[j, :, at], preferred_element_type=f32)
            for b in range(tile // LANES):
                rows = pl.ds(pl.multiple_of((t * (tile // LANES) + b) * width, width), width)
                target[rows, :] = y[:, b * LANES : (b + 1) * LANES].astype(target.dtype)
            return carry

        lax.fori_loop(0, span // tile, step, 0)

    def copy_a(q):
        return remote(send_a.at[q], recv_a.at[q], sa.at[q], ra.at[q], partner)

    def copy_b(q, k):
        to = lax.rem(chip + k, chips)
        rows = pl.ds(pl.multiple_of(to * rows_b, rows_b), rows_b)
        return remote(
            send_b.at[q, rows, :], recv_b.at[q, k - 1], sb.at[q, k - 1], rb.at[q, k - 1], in_plane(k)
        )

    def copy_c(q, k):
        to = lax.rem(z + k, n_dp)
        rows = pl.ds(pl.multiple_of(to * rows_c, rows_c), rows_c)
        return remote(
            acc_b.at[q, rows, :], recv_c.at[q, k - 1], sc.at[q, k - 1], rc.at[q, k - 1], in_line(k)
        )

    def copy_d(q, k):
        rows = pl.ds(pl.multiple_of(chip * rows_b + z * rows_c, rows_c), rows_c)
        piece = full.at[core, q, rows, :]
        return remote(piece, piece, sd.at[q, k - 1], rd.at[q, k - 1], in_line(k))

    def copy_e(q, k):
        rows = pl.ds(pl.multiple_of(chip * rows_b, rows_b), rows_b)
        piece = full.at[core, q, rows, :]
        return remote(piece, piece, se.at[q, k - 1], re.at[q, k - 1], in_plane(k))

    def copy_f(q):
        piece = full.at[core, q]
        return remote(piece, piece, sf.at[q], rf.at[q], partner)

    for q in range(split):
        product(q, send_a.at[q])
        copy_a(q).start()
    for q in range(split):
        product(split + q, acc_a.at[q])
    plane = range(1, chips)
    line = range(1, n_dp)
    for q in range(split):
        copy_a(q).wait_recv()
        acc_a[q] = acc_a[q] + recv_a[q].astype(f32)
        send_b[q] = acc_a[q].astype(bf16)
        for k in plane:
            copy_b(q, k).start()
    for q in range(split):
        own = pl.ds(pl.multiple_of(chip * rows_b, rows_b), rows_b)
        total = acc_a[q, own, :]
        for k in plane:
            copy_b(q, k).wait_recv()
            total = total + recv_b[q, k - 1].astype(f32)
        acc_b[q] = total
        for k in line:
            copy_c(q, k).start()
    for q in range(split):
        own = pl.ds(pl.multiple_of(z * rows_c, rows_c), rows_c)
        total = acc_b[q, own, :]
        for k in line:
            copy_c(q, k).wait_recv()
            total = total + recv_c[q, k - 1]
        rows = pl.ds(pl.multiple_of(chip * rows_b + z * rows_c, rows_c), rows_c)
        full[core, q, rows, :] = (total * scaling).astype(bf16)
        for k in line:
            copy_d(q, k).start()
    for q in range(split):
        for k in line:
            copy_d(q, k).wait_recv()
        for k in plane:
            copy_e(q, k).start()
    for q in range(split):
        for k in plane:
            copy_e(q, k).wait_recv()
        copy_f(q).start()

    def unpack(side, q):
        for b in range(span // LANES):
            at = pl.ds(pl.multiple_of(side * half + q * span + b * LANES, LANES), LANES)
            out_ref[:, at] = full[side, q, pl.ds(b * width, width), :]

    for q in range(split):
        unpack(core, q)
    for q in range(split):
        copy_f(q).wait_recv()
        unpack(1 - core, q)
    each(lambda k: copy_grads(k).wait_recv())
    incoming_ref[...] = arrived[...].astype(f32)
    each(lambda k: copy_asks(k).wait_send())
    each(lambda k: copy_rows(k).wait_send())
    each(lambda k: copy_grads(k).wait_send())
    for q in range(split):
        copy_a(q).wait_send()
        copy_f(q).wait_send()
        for k in plane:
            copy_b(q, k).wait_send()
            copy_e(q, k).wait_send()
        for k in line:
            copy_c(q, k).wait_send()
            copy_d(q, k).wait_send()


def reduce_terms(asked, slot_index, projection, cotangent, table, capacity, scaling):
    n_vocab, n_dp = lax.axis_size("vocab"), lax.axis_size("dp")
    tokens = slot_index.shape[0]
    held_rows, width = table.shape
    devices_all = n_vocab * n_dp
    slots = devices_all * capacity
    hidden_width = cotangent.shape[1]
    split = 2
    chips = n_vocab // 2
    span = hidden_width // (2 * split)
    rows_a = width * span // LANES
    rows_b = rows_a // chips
    rows_c = rows_b // n_dp
    f32, bf16 = jnp.float32, jnp.bfloat16
    dma = pltpu.SemaphoreType.DMA
    plane, line = max(1, chips - 1), max(1, n_dp - 1)
    return pl.pallas_call(
        functools.partial(reduce_kernel, n_vocab, n_dp, split, scaling),
        out_shape=[
            jax.ShapeDtypeStruct((width, hidden_width), bf16),
            jax.ShapeDtypeStruct((tokens, width), bf16),
            jax.ShapeDtypeStruct((slots, width), f32),
            jax.ShapeDtypeStruct(asked.shape, jnp.int32),
        ],
        in_specs=[pl.BlockSpec(memory_space=pltpu.VMEM)] * 4
        + [pl.BlockSpec(memory_space=pl.ANY)] * 2,
        out_specs=[pl.BlockSpec(memory_space=pltpu.VMEM)] * 4,
        scratch_shapes=[
            pltpu.VMEM(asked.shape, jnp.int32),
            pltpu.SMEM(asked.shape, jnp.int32),
            pltpu.VMEM((held_rows, width), bf16),
            pltpu.VMEM((held_rows, width), f32),
            pltpu.VMEM((capacity, width), f32),
            pltpu.VMEM((slots, width), bf16),
            dma, dma,
            dma((devices_all,)), dma((devices_all,)),
            pltpu.VMEM((slots, width), bf16),
            pltpu.VMEM((slots, width), bf16),
            pltpu.VMEM((slots, width), bf16),
            pltpu.VMEM((tokens, width), f32),
            pltpu.VMEM((tokens, width), bf16),
            dma((devices_all,)), dma((devices_all,)),
            dma((devices_all,)), dma((devices_all,)),
            pltpu.VMEM((2 * split, tokens, span), bf16),
            pltpu.VMEM((width, tokens), bf16),
            pltpu.VMEM((split, rows_a, LANES), bf16),
            pltpu.VMEM((split, rows_a, LANES), bf16),
            pltpu.VMEM((split, rows_a, LANES), f32),
            pltpu.VMEM((split, rows_a, LANES), bf16),
            pltpu.VMEM((split, plane, rows_b, LANES), bf16),
            pltpu.VMEM((split, rows_b, LANES), f32),
            pltpu.VMEM((split, line, rows_c, LANES), f32),
            pltpu.VMEM((2, split, rows_a, LANES), bf16),
            dma((2 * split,)),
            dma((split,)), dma((split,)),
            dma((split, plane)), dma((split, plane)),
            dma((split, line)), dma((split, line)),
            dma((split, line)), dma((split, line)),
            dma((split, plane)), dma((split, plane)),
            dma((split,)), dma((split,)),
        ],
        compiler_params=pltpu.CompilerParams(collective_id=1, has_side_effects=True),
        name="reduce_terms",
    )(asked, slot_index[None, :], slot_index[:, None], projection, cotangent, table)


def body(token_ids, counts, table, projection, cotangent):
    tokens_here = token_ids.shape[0]
    held_rows = table.shape[0]
    width = table.shape[1]
    hidden_width = projection.shape[1]
    devices_all = lax.axis_size("vocab") * lax.axis_size("dp")
    capacity = max(4, 2 * tokens_here // devices_all)
    slots = devices_all * capacity
    bf16, f32 = jnp.bfloat16, jnp.float32

    owner = token_ids // held_rows
    local_row = token_ids - owner * held_rows
    hits = (owner[:, None] == jnp.arange(devices_all, dtype=jnp.int32)[None, :]).astype(bf16)
    order = jnp.arange(tokens_here, dtype=jnp.int32)
    before = (order[:, None] >= order[None, :]).astype(bf16)
    ranks = jnp.dot(before, hits, preferred_element_type=f32)
    rank = jnp.sum(ranks * hits.astype(f32), axis=1).astype(jnp.int32) - 1
    slot_index = jnp.where(order < counts[0], owner * capacity + rank, -1)
    place = (slot_index[:, None] == jnp.arange(slots, dtype=jnp.int32)[None, :]).astype(bf16)
    digits = jnp.stack(
        [local_row // 65536, (local_row // 256) % 256, local_row % 256, jnp.ones_like(local_row)]
    ).astype(bf16)
    found = jnp.dot(digits, place, preferred_element_type=f32).astype(jnp.int32)
    requests = found[0] * 65536 + found[1] * 256 + found[2] + found[3] - 1
    requests = jnp.where(found[3] > 0, requests, -1)

    asked = jnp.pad(
        requests.reshape(devices_all, 1, capacity),
        ((0, 0), (0, 0), (0, -capacity % LANES)),
        constant_values=-1,
    )
    scaling = 1.0 / math.sqrt(tokens_here * devices_all)
    terms, embedded, incoming, wanted = reduce_terms(
        asked, slot_index, projection, cotangent, table, capacity, scaling
    )
    grad_table, hidden, grad_projection = finish(
        wanted, incoming, embedded, projection, terms, held_rows, capacity
    )
    return (hidden, grad_projection, grad_table)


def solution(mesh):
    return jax.shard_map(
        body,
        mesh=mesh,
        in_specs=(
            P(AXES),
            P(AXES),
            P(AXES, None),
            P(),
            P(AXES, None),
        ),
        out_specs=(P(AXES, None), P(), P(AXES, None)),
        check_vma=False,
    )
```

```python
import functools
import math

import jax
import jax.numpy as jnp
from jax import lax
from jax.experimental import pallas as pl
from jax.experimental.pallas import tpu as pltpu
from jax.sharding import PartitionSpec as P

AXES = ("vocab", "dp")
ACCS = 4


def finish_kernel(
    capacity, chunks, wanted_ref, incoming_ref, emb_ref, proj_ref, terms_ref,
    table_out, hidden_out, proj_out,
    acc0, acc1, acc2, acc3, hid, grad, table_sems, hidden_sems, proj_sem,
):
    f32, bf16 = jnp.float32, jnp.bfloat16
    accs = (acc0, acc1, acc2, acc3)
    held, width = acc0.shape
    part = held // chunks
    slots = incoming_ref.shape[0]
    tokens, hidden_width = hid.shape
    high, wide = min(512, tokens), min(256, hidden_width)
    blocks, tiles = tokens // high, hidden_width // wide
    per = slots // (blocks * tiles)
    group = min(8, per, capacity)

    def convert(i, carry):
        at = pl.ds(pl.multiple_of(i * wide, wide), wide)
        grad[:, at] = terms_ref[:, at].astype(f32)
        return carry

    lax.fori_loop(0, tiles, convert, 0)
    proj_copy = pltpu.make_async_copy(grad, proj_out, proj_sem)
    proj_copy.start()

    def clear(i, carry):
        at = pl.ds(pl.multiple_of(i * 64, 64), 64)
        for acc in accs:
            acc[at, :] = jnp.zeros((64, width), f32)
        return carry

    lax.fori_loop(0, held // 64, clear, 0)

    def hidden_copy(r):
        at = pl.ds(r * high, high)
        return pltpu.make_async_copy(hid.at[at, :], hidden_out.at[at, :], hidden_sems.at[r])

    for r in range(blocks):

        def step(t, carry):
            at = pl.ds(pl.multiple_of(t * wide, wide), wide)
            y = jnp.dot(emb_ref[r * high : (r + 1) * high, :], proj_ref[:, at], preferred_element_type=f32)
            start = (r * tiles + t) * per
            for g in range(per // group):
                base = pl.multiple_of(start + g * group, group)
                block = incoming_ref[pl.ds(base, group), :]
                source = base // capacity
                first = lax.rem(base, capacity)
                for j in range(group):
                    acc = accs[j % ACCS]
                    row = pl.ds(jnp.maximum(wanted_ref[source, 0, first + j], 0), 1)
                    acc[row, :] = acc[row, :] + block[j : j + 1, :]
            hid[r * high : (r + 1) * high, at] = y.astype(bf16)
            return carry

        lax.fori_loop(0, tiles, step, 0)
        hidden_copy(r).start()

    def table_copy(c):
        at = pl.ds(c * part, part)
        return pltpu.make_async_copy(acc0.at[at, :], table_out.at[at, :], table_sems.at[c])

    for c in range(chunks):

        def join(i, carry):
            at = pl.ds(pl.multiple_of(c * part + i * 64, 64), 64)
            acc0[at, :] = (acc0[at, :] + acc1[at, :]) + (acc2[at, :] + acc3[at, :])
            return carry

        lax.fori_loop(0, part // 64, join, 0)
        table_copy(c).start()
    proj_copy.wait()
    for r in range(blocks):
        hidden_copy(r).wait()
    for c in range(chunks):
        table_copy(c).wait()


def finish(wanted, incoming, embedded, projection, terms, held_rows, capacity):
    tokens, width = embedded.shape
    hidden_width = projection.shape[1]
    chunks = 8
    f32, bf16 = jnp.float32, jnp.bfloat16
    dma = pltpu.SemaphoreType.DMA
    return pl.pallas_call(
        functools.partial(finish_kernel, capacity, chunks),
        out_shape=[
            jax.ShapeDtypeStruct((held_rows, width), f32),
            jax.ShapeDtypeStruct((tokens, hidden_width), bf16),
            jax.ShapeDtypeStruct((width, hidden_width), f32),
        ],
        in_specs=[pl.BlockSpec(memory_space=pltpu.SMEM)]
        + [pl.BlockSpec(memory_space=pltpu.VMEM)] * 4,
        out_specs=[pl.BlockSpec(memory_space=pl.ANY)] * 3,
        scratch_shapes=[pltpu.VMEM((held_rows, width), f32)] * ACCS
        + [
            pltpu.VMEM((tokens, hidden_width), bf16),
            pltpu.VMEM((width, hidden_width), f32),
            dma((chunks,)),
            dma((tokens // min(512, tokens),)),
            dma,
        ],
        name="finish",
    )(wanted, incoming, embedded, projection, terms)


MESH = pl.DeviceIdType.MESH
LANES = 128


def remote(src, dst, send_sem, recv_sem, where):
    return pltpu.make_async_remote_copy(
        src_ref=src, dst_ref=dst, send_sem=send_sem, recv_sem=recv_sem,
        device_id=where, device_id_type=MESH,
    )


def reduce_kernel(
    n_vocab, n_dp, split, scaling,
    asked_ref, slot_row, slot_col, proj_ref, cot_ref, table_ref,
    out_ref, emb_ref, incoming_ref, wanted_ref,
    wanted, wanted_s, table_half, table_full, stage, picked, table_sem, want_sem, asks_s, asks_r,
    returned, outgoing, arrived, grad_sum, grad_half, rows_s, rows_r, grads_s, grads_r,
    cot_buf, emb_t, send_a, recv_a, acc_a, send_b, recv_b, acc_b, recv_c, full,
    load_sem, sa, ra, sb, rb, sc, rc, sd, rd, se, re, sf, rf,
):
    f32, bf16 = jnp.float32, jnp.bfloat16
    v = lax.axis_index("vocab")
    z = lax.axis_index("dp")
    core, chip = lax.rem(v, 2), v // 2
    chips = n_vocab // 2
    width, hidden_width = out_ref.shape
    half = hidden_width // 2
    span = half // split
    rows_a = width * span // LANES
    rows_b = rows_a // chips
    rows_c = rows_b // n_dp
    tile = min(256, span)
    partner = (chip * 2 + 1 - core, z)

    def in_plane(k):
        return (lax.rem(chip + k, chips) * 2 + core, z)

    def in_line(k):
        return (v, lax.rem(z + k, n_dp))

    def load(j):
        side = (1 - core) if j < split else core
        at = pl.ds(pl.multiple_of(side * half + (j % split) * span, LANES), span)
        return pltpu.make_async_copy(cot_ref.at[:, at], cot_buf.at[j], load_sem.at[j])

    table_load = pltpu.make_async_copy(table_ref, table_half, table_sem)
    table_load.start()
    for j in range(2 * split):
        load(j).start()
    devices_all = n_vocab * n_dp
    me = v * n_dp + z
    tokens = slot_row.shape[1]
    slots = returned.shape[0]
    capacity = slots // devices_all
    barrier = pltpu.get_barrier_semaphore()

    def device(k):
        to = lax.rem(me + k, devices_all)
        return to, (to // n_dp, lax.rem(to, n_dp))

    def greet(k, carry):
        pl.semaphore_signal(barrier, inc=1, device_id=device(k)[1], device_id_type=MESH)
        return carry

    def block(at):
        return pl.ds(pl.multiple_of(at * capacity, capacity), capacity)

    def copy_asks(k):
        to, where = device(k)
        return remote(asked_ref.at[to], wanted.at[me], asks_s.at[k], asks_r.at[k], where)

    def copy_rows(k):
        to, where = device(k)
        return remote(
            picked.at[block(to), :], returned.at[block(me), :], rows_s.at[k], rows_r.at[k], where
        )

    def copy_grads(k):
        to, where = device(k)
        return remote(
            outgoing.at[block(to), :], arrived.at[block(me), :], grads_s.at[k], grads_r.at[k], where
        )

    def each(action):
        def step(k, carry):
            action(k)
            return carry

        lax.fori_loop(1, devices_all, step, 0)

    lax.fori_loop(1, devices_all, greet, 0)
    pl.semaphore_wait(barrier, devices_all - 1)
    each(lambda k: copy_asks(k).start())
    wanted[me] = asked_ref[me]
    table_load.wait()
    held_rows = table_half.shape[0]
    wide = min(256, held_rows)

    def widen(i, carry):
        rows = pl.ds(pl.multiple_of(i * wide, wide), wide)
        table_full[rows, :] = table_half[rows, :].astype(f32)
        return carry

    lax.fori_loop(0, held_rows // wide, widen, 0)
    each(lambda k: copy_asks(k).wait_recv())
    to_scalars = pltpu.make_async_copy(wanted, wanted_s, want_sem)
    to_scalars.start()
    to_scalars.wait()

    def pick(at):
        for i in range(capacity):
            row = jnp.maximum(wanted_s[at, 0, i], 0)
            stage[i : i + 1, :] = table_full[pl.ds(row, 1), :]
        return stage[...].astype(bf16)

    def serve(k):
        at = device(k)[0]
        picked[block(at), :] = pick(at)
        copy_rows(k).start()

    each(serve)
    returned[block(me), :] = pick(me)
    wanted_ref[...] = wanted[...]

    rows_tile = min(256, tokens)
    for j in range(2 * split):
        load(j).wait()
        side = (1 - core) if j < split else core
        at = pl.ds(pl.multiple_of(side * half + (j % split) * span, LANES), span)

        def back(t, carry):
            rows = pl.ds(pl.multiple_of(t * rows_tile, rows_tile), rows_tile)
            y = lax.dot_general(
                cot_buf[j, rows, :], proj_ref[:, at], (((1,), (1,)), ((), ())),
                preferred_element_type=f32,
            )
            if j == 0:
                grad_sum[rows, :] = y
            else:
                grad_sum[rows, :] = grad_sum[rows, :] + y
            return carry

        lax.fori_loop(0, tokens // rows_tile, back, 0)
    grad_half[...] = grad_sum[...].astype(bf16)

    slot_tile = 256

    def spread(t, carry):
        base = pl.multiple_of(t * slot_tile, slot_tile)
        ids = lax.broadcasted_iota(jnp.int32, (slot_tile, tokens), 0) + base
        place = jnp.where(ids == slot_row[...], 1.0, 0.0).astype(bf16)
        y = jnp.dot(place, grad_half[...], preferred_element_type=f32)
        outgoing[pl.ds(base, slot_tile), :] = y.astype(bf16)
        return carry

    lax.fori_loop(0, slots // slot_tile, spread, 0)
    each(lambda k: copy_grads(k).start())
    arrived[block(me), :] = outgoing[block(me), :]
    each(lambda k: copy_rows(k).wait_recv())

    def embed(t, carry):
        rows = pl.ds(pl.multiple_of(t * rows_tile, rows_tile), rows_tile)
        ids = lax.broadcasted_iota(jnp.int32, (rows_tile, slots), 1)
        place = jnp.where(ids == slot_col[rows, :], 1.0, 0.0).astype(bf16)
        y = jnp.dot(place, returned[...], preferred_element_type=f32)
        emb_ref[rows, :] = y.astype(bf16)
        return carry

    lax.fori_loop(0, tokens // rows_tile, embed, 0)
    emb_t[...] = emb_ref[...].T

    def product(j, target):
        def step(t, carry):
            at = pl.ds(pl.multiple_of(t * tile, tile), tile)
            y = jnp.dot(emb_t[...], cot_buf[j, :, at], preferred_element_type=f32)
            for b in range(tile // LANES):
                rows = pl.ds(pl.multiple_of((t * (tile // LANES) + b) * width, width), width)
                target[rows, :] = y[:, b * LANES : (b + 1) * LANES].astype(target.dtype)
            return carry

        lax.fori_loop(0, span // tile, step, 0)

    def copy_a(q):
        return remote(send_a.at[q], recv_a.at[q], sa.at[q], ra.at[q], partner)

    def copy_b(q, k):
        to = lax.rem(chip + k, chips)
        rows = pl.ds(pl.multiple_of(to * rows_b, rows_b), rows_b)
        return remote(
            send_b.at[q, rows, :], recv_b.at[q, k - 1], sb.at[q, k - 1], rb.at[q, k - 1], in_plane(k)
        )

    def copy_c(q, k):
        to = lax.rem(z + k, n_dp)
        rows = pl.ds(pl.multiple_of(to * rows_c, rows_c), rows_c)
        return remote(
            acc_b.at[q, rows, :], recv_c.at[q, k - 1], sc.at[q, k - 1], rc.at[q, k - 1], in_line(k)
        )

    def copy_d(q, k):
        rows = pl.ds(pl.multiple_of(chip * rows_b + z * rows_c, rows_c), rows_c)
        piece = full.at[core, q, rows, :]
        return remote(piece, piece, sd.at[q, k - 1], rd.at[q, k - 1], in_line(k))

    def copy_e(q, k):
        rows = pl.ds(pl.multiple_of(chip * rows_b, rows_b), rows_b)
        piece = full.at[core, q, rows, :]
        return remote(piece, piece, se.at[q, k - 1], re.at[q, k - 1], in_plane(k))

    def copy_f(q):
        piece = full.at[core, q]
        return remote(piece, piece, sf.at[q], rf.at[q], partner)

    for q in range(split):
        product(q, send_a.at[q])
        copy_a(q).start()
    for q in range(split):
        product(split + q, acc_a.at[q])
    plane = range(1, chips)
    line = range(1, n_dp)
    for q in range(split):
        copy_a(q).wait_recv()
        acc_a[q] = acc_a[q] + recv_a[q].astype(f32)
        send_b[q] = acc_a[q].astype(bf16)
        for k in plane:
            copy_b(q, k).start()
    for q in range(split):
        own = pl.ds(pl.multiple_of(chip * rows_b, rows_b), rows_b)
        total = acc_a[q, own, :]
        for k in plane:
            copy_b(q, k).wait_recv()
            total = total + recv_b[q, k - 1].astype(f32)
        acc_b[q] = total
        for k in line:
            copy_c(q, k).start()
    for q in range(split):
        own = pl.ds(pl.multiple_of(z * rows_c, rows_c), rows_c)
        total = acc_b[q, own, :]
        for k in line:
            copy_c(q, k).wait_recv()
            total = total + recv_c[q, k - 1]
        rows = pl.ds(pl.multiple_of(chip * rows_b + z * rows_c, rows_c), rows_c)
        full[core, q, rows, :] = (total * scaling).astype(bf16)
        for k in line:
            copy_d(q, k).start()
    for q in range(split):
        for k in line:
            copy_d(q, k).wait_recv()
        for k in plane:
            copy_e(q, k).start()
    for q in range(split):
        for k in plane:
            copy_e(q, k).wait_recv()
        copy_f(q).start()

    def unpack(side, q):
        for b in range(span // LANES):
            at = pl.ds(pl.multiple_of(side * half + q * span + b * LANES, LANES), LANES)
            out_ref[:, at] = full[side, q, pl.ds(b * width, width), :]

    for q in range(split):
        unpack(core, q)
    for q in range(split):
        copy_f(q).wait_recv()
        unpack(1 - core, q)
    each(lambda k: copy_grads(k).wait_recv())
    incoming_ref[...] = arrived[...].astype(f32)
    each(lambda k: copy_asks(k).wait_send())
    each(lambda k: copy_rows(k).wait_send())
    each(lambda k: copy_grads(k).wait_send())
    for q in range(split):
        copy_a(q).wait_send()
        copy_f(q).wait_send()
        for k in plane:
            copy_b(q, k).wait_send()
            copy_e(q, k).wait_send()
        for k in line:
            copy_c(q, k).wait_send()
            copy_d(q, k).wait_send()


def reduce_terms(asked, slot_index, projection, cotangent, table, capacity, scaling):
    n_vocab, n_dp = lax.axis_size("vocab"), lax.axis_size("dp")
    tokens = slot_index.shape[0]
    held_rows, width = table.shape
    devices_all = n_vocab * n_dp
    slots = devices_all * capacity
    hidden_width = cotangent.shape[1]
    split = 2
    chips = n_vocab // 2
    span = hidden_width // (2 * split)
    rows_a = width * span // LANES
    rows_b = rows_a // chips
    rows_c = rows_b // n_dp
    f32, bf16 = jnp.float32, jnp.bfloat16
    dma = pltpu.SemaphoreType.DMA
    plane, line = max(1, chips - 1), max(1, n_dp - 1)
    return pl.pallas_call(
        functools.partial(reduce_kernel, n_vocab, n_dp, split, scaling),
        out_shape=[
            jax.ShapeDtypeStruct((width, hidden_width), bf16),
            jax.ShapeDtypeStruct((tokens, width), bf16),
            jax.ShapeDtypeStruct((slots, width), f32),
            jax.ShapeDtypeStruct(asked.shape, jnp.int32),
        ],
        in_specs=[pl.BlockSpec(memory_space=pltpu.VMEM)] * 4
        + [pl.BlockSpec(memory_space=pl.ANY)] * 2,
        out_specs=[pl.BlockSpec(memory_space=pltpu.VMEM)] * 4,
        scratch_shapes=[
            pltpu.VMEM(asked.shape, jnp.int32),
            pltpu.SMEM(asked.shape, jnp.int32),
            pltpu.VMEM((held_rows, width), bf16),
            pltpu.VMEM((held_rows, width), f32),
            pltpu.VMEM((capacity, width), f32),
            pltpu.VMEM((slots, width), bf16),
            dma, dma,
            dma((devices_all,)), dma((devices_all,)),
            pltpu.VMEM((slots, width), bf16),
            pltpu.VMEM((slots, width), bf16),
            pltpu.VMEM((slots, width), bf16),
            pltpu.VMEM((tokens, width), f32),
            pltpu.VMEM((tokens, width), bf16),
            dma((devices_all,)), dma((devices_all,)),
            dma((devices_all,)), dma((devices_all,)),
            pltpu.VMEM((2 * split, tokens, span), bf16),
            pltpu.VMEM((width, tokens), bf16),
            pltpu.VMEM((split, rows_a, LANES), bf16),
            pltpu.VMEM((split, rows_a, LANES), bf16),
            pltpu.VMEM((split, rows_a, LANES), f32),
            pltpu.VMEM((split, rows_a, LANES), bf16),
            pltpu.VMEM((split, plane, rows_b, LANES), bf16),
            pltpu.VMEM((split, rows_b, LANES), f32),
            pltpu.VMEM((split, line, rows_c, LANES), f32),
            pltpu.VMEM((2, split, rows_a, LANES), bf16),
            dma((2 * split,)),
            dma((split,)), dma((split,)),
            dma((split, plane)), dma((split, plane)),
            dma((split, line)), dma((split, line)),
            dma((split, line)), dma((split, line)),
            dma((split, plane)), dma((split, plane)),
            dma((split,)), dma((split,)),
        ],
        compiler_params=pltpu.CompilerParams(collective_id=1, has_side_effects=True),
        name="reduce_terms",
    )(asked, slot_index[None, :], slot_index[:, None], projection, cotangent, table)


def body(token_ids, counts, table, projection, cotangent):
    tokens_here = token_ids.shape[0]
    held_rows = table.shape[0]
    width = table.shape[1]
    hidden_width = projection.shape[1]
    devices_all = lax.axis_size("vocab") * lax.axis_size("dp")
    capacity = max(4, 2 * tokens_here // devices_all)
    slots = devices_all * capacity
    bf16, f32 = jnp.bfloat16, jnp.float32

    owner = token_ids // held_rows
    local_row = token_ids - owner * held_rows
    hits = (owner[:, None] == jnp.arange(devices_all, dtype=jnp.int32)[None, :]).astype(bf16)
    order = jnp.arange(tokens_here, dtype=jnp.int32)
    before = (order[:, None] >= order[None, :]).astype(bf16)
    ranks = jnp.dot(before, hits, preferred_element_type=f32)
    rank = jnp.sum(ranks * hits.astype(f32), axis=1).astype(jnp.int32) - 1
    slot_index = jnp.where(order < counts[0], owner * capacity + rank, -1)
    place = (slot_index[:, None] == jnp.arange(slots, dtype=jnp.int32)[None, :]).astype(bf16)
    digits = jnp.stack(
        [local_row // 65536, (local_row // 256) % 256, local_row % 256, jnp.ones_like(local_row)]
    ).astype(bf16)
    found = jnp.dot(digits, place, preferred_element_type=f32).astype(jnp.int32)
    requests = found[0] * 65536 + found[1] * 256 + found[2] + found[3] - 1
    requests = jnp.where(found[3] > 0, requests, -1)

    asked = jnp.pad(
        requests.reshape(devices_all, 1, capacity),
        ((0, 0), (0, 0), (0, -capacity % LANES)),
        constant_values=-1,
    )
    scaling = 1.0 / math.sqrt(tokens_here * devices_all)
    terms, embedded, incoming, wanted = reduce_terms(
        asked, slot_index, projection, cotangent, table, capacity, scaling
    )
    grad_table, hidden, grad_projection = finish(
        wanted, incoming, embedded, projection, terms, held_rows, capacity
    )
    return (hidden, grad_projection, grad_table)


def solution(mesh):
    return jax.shard_map(
        body,
        mesh=mesh,
        in_specs=(
            P(AXES),
            P(AXES),
            P(AXES, None),
            P(),
            P(AXES, None),
        ),
        out_specs=(P(AXES, None), P(), P(AXES, None)),
        check_vma=False,
    )
```
